128 devices in a mesh: sec: 4 (over x_hi, core), space: 32 (over z, x_lo, y).
Axes of the slice: x: 4 (x_hi: 2, x_lo: 2; x = x_hi * 2 + x_lo), y: 4, z: 4, core: 2. Of those that a mesh axis runs over, the one named last changes fastest.
Arguments:
- droplet_integrals: float32 [64, 5, 256, 2048], P('sec', None, 'space'), may hold values from -3 to 3, as said below
- flow_number_lengthwise: float32 [64], P('sec'), may hold values from -0.6 to 0.6
- flow_number_crosswise: float32 [64], P('sec'), may hold values from -0.35 to 0.35
- inflow_boundary_integrals: float32 [64, 5], P('sec'), may hold values from 0.2 to 2
- boundary_wall_indicator: int32 [256, 2048], P('space'), may hold values 0 or 1
- inflow_indicator: int32 [256, 2048], P('space'), may hold values 0 or 1
- collision_coefficient: float32 [64, 64], replicated, may hold values from 0.0005 to 0.008
- collision_target_share: float32 [64, 64], replicated, may hold values from 0 to 0.03
- evaporation_speed_stepwise: float32 [64], replicated, may hold values from 0.01 to 0.1
- thermal_factor: float32 [256, 2048], P('space', 'sec'), may hold values from 0.5 to 2
Outputs:
- spray: float32 [64, 5, 256, 2048], P(None, None, 'space', 'sec')
- gas_source: float32 [5, 256, 2048], P(None, 'space', 'sec')
The draws below stay inside these ranges and needn't reach their ends.
Inputs may be any that keep to these rules, and one draw needn't show every extreme that they name: `droplet_integrals`: moment 0 (mass) is positive, 0.1 or more, in every section and cell.
All inputs are finite; a program needn't handle non-finite values. No bound on the sum of `boundary_wall_indicator` or of `inflow_indicator` on one device may be relied on, other than what follows from the above.
Results may differ from the reference program's by a relative error of at most 0.000084.
Values sent between devices are 32-bit elements; how exact they have to be, the bound alone decides.
A program may use at most 128 MiB of HBM per device.

```python
import math
import jax
import jax.numpy as jnp
from jax import lax

SECTIONS = 64
MOM = 5
SUB = 4
GRID_COLUMN_SPAN = 2048
GRID_ROWS_COUNT = 256


def draw_droplet_integrals(key, part):
    mass_key, rest_key = jax.random.split(jax.random.fold_in(key, 11))
    mass_part = jnp.exp(jax.random.uniform(mass_key, (SECTIONS, 1, GRID_ROWS_COUNT, GRID_COLUMN_SPAN), jnp.float32, math.log(0.2), math.log(2.0)))
    rest_part = jnp.clip(0.5 * jax.random.normal(rest_key, (SECTIONS, MOM - 1, GRID_ROWS_COUNT, GRID_COLUMN_SPAN), jnp.float32), -3.0, 3.0)
    return jnp.concatenate([mass_part, rest_part], axis=1)


def plant(array, rng, least, largest):
    spot = [jax.random.randint(jax.random.fold_in(rng, axis), (), 0, length) for axis, length in enumerate(array.shape)]
    widest = array.shape.index(max(array.shape))
    neighbour = spot[:widest] + [(spot[widest] + 1) % array.shape[widest]] + spot[widest + 1:]
    return array.at[tuple(spot)].set(least).at[tuple(neighbour)].set(largest)


def shard_levels(rng, extent, pieces, smallest, largest):
    gain, own = 1.0, jax.random.fold_in(rng, 6)
    for position, blocks in pieces:
        steps = jnp.exp(jax.random.uniform(jax.random.fold_in(own, position), (blocks,), jnp.float32, smallest / len(pieces), largest / len(pieces)))
        gain = gain * jnp.repeat(steps, extent[position] // blocks).reshape([-1 if axis == position else 1 for axis in range(len(extent))])
    return gain


def setup_inputs(seed: int = 0) -> dict:
    splits = jax.random.split(jax.random.key(seed), 11)
    droplet_integrals = draw_droplet_integrals(jax.random.fold_in(splits[10], 71), 0)
    flow_number_lengthwise = jnp.clip(jax.random.uniform(splits[1], (SECTIONS,), jnp.float32, -0.6, 0.6) * shard_levels(splits[1], (SECTIONS,), ((0, 4),), -0.4, 0.0), -0.6, 0.6)
    flow_number_crosswise = jnp.clip(jax.random.uniform(splits[2], (SECTIONS,), jnp.float32, -0.35, 0.35) * shard_levels(splits[2], (SECTIONS,), ((0, 4),), -0.4, 0.0), -0.35, 0.35)
    inflow_boundary_integrals = jnp.clip(0.2 + 1.8 * jax.random.uniform(splits[3], (SECTIONS, MOM), jnp.float32) ** shard_levels(splits[3], (SECTIONS, MOM), ((0, 4),), -0.2, 0.2), 0.2, 2.0)
    boundary_wall_indicator = plant((jax.random.randint(splits[4], (GRID_ROWS_COUNT, GRID_COLUMN_SPAN), 0, 16) < 1).astype(jnp.int32), jax.random.fold_in(splits[4], 1), 0, 1)
    inflow_indicator = plant((jax.random.randint(splits[5], (GRID_ROWS_COUNT, GRID_COLUMN_SPAN), 0, 32) < 1).astype(jnp.int32), jax.random.fold_in(splits[5], 1), 0, 1)
    collision_coefficient = jnp.clip(jnp.exp(jax.random.uniform(splits[6], (SECTIONS, SECTIONS), jnp.float32, math.log(0.0005), math.log(0.008))), 0.0005, 0.008)
    collision_target_share = jnp.clip(jax.random.uniform(splits[7], (SECTIONS, SECTIONS), jnp.float32, 0.0, 0.03), 0.0, 0.03)
    evaporation_speed_stepwise = jnp.clip(jnp.exp(jax.random.uniform(splits[8], (SECTIONS,), jnp.float32, math.log(0.01), math.log(0.1))), 0.01, 0.1)
    thermal_factor = jnp.clip(jnp.exp(math.log(2.0) - 1.3862944 * jax.random.uniform(splits[9], (GRID_ROWS_COUNT, GRID_COLUMN_SPAN), jnp.float32) ** shard_levels(splits[9], (GRID_ROWS_COUNT, GRID_COLUMN_SPAN), ((0, 32), (1, 4)), -0.2, 0.2)), 0.5, 2.0)
    return dict(droplet_integrals=droplet_integrals, flow_number_lengthwise=flow_number_lengthwise, flow_number_crosswise=flow_number_crosswise, inflow_boundary_integrals=inflow_boundary_integrals, boundary_wall_indicator=boundary_wall_indicator, inflow_indicator=inflow_indicator, collision_coefficient=collision_coefficient, collision_target_share=collision_target_share, evaporation_speed_stepwise=evaporation_speed_stepwise, thermal_factor=thermal_factor)


def advance(padded, speed_x, speed_y, inflow_value, inflow_rows, wall_rows):
    middle = padded[..., 1:-1, :]
    western = padded[..., :-2, :]
    eastern = padded[..., 2:, :]
    border = jnp.zeros_like(middle[..., :1])
    southern = jnp.concatenate([border, middle[..., :-1]], axis=-1)
    northern = jnp.concatenate([middle[..., 1:], border], axis=-1)
    transported_integrals = middle - jnp.maximum(speed_x, 0.0) * (middle - western) - jnp.minimum(speed_x, 0.0) * (eastern - middle)
    transported_integrals = transported_integrals - jnp.maximum(speed_y, 0.0) * (middle - southern) - jnp.minimum(speed_y, 0.0) * (northern - middle)
    transported_integrals = jnp.where(inflow_rows > 0, inflow_value, transported_integrals)
    return jnp.where(wall_rows > 0, jnp.zeros_like(transported_integrals), transported_integrals)


def couple(cell_block, collision_coefficient, collision_target_share):
    mass_part = cell_block[:, 0]
    merge_rate = jnp.einsum("sj,jxy->sxy", collision_coefficient, mass_part, precision=lax.Precision.HIGHEST)
    flux_terms = cell_block * merge_rate[:, None]
    gained = jnp.einsum("sj,jmxy->smxy", collision_target_share, flux_terms, precision=lax.Precision.HIGHEST)
    return cell_block - flux_terms + gained


def reference(droplet_integrals, flow_number_lengthwise, flow_number_crosswise, inflow_boundary_integrals, boundary_wall_indicator, inflow_indicator, collision_coefficient, collision_target_share, evaporation_speed_stepwise, thermal_factor):
    def move_one(items):
        field, speed_x, speed_y, inflow_row = items
        for substep in range(SUB):
            padded = jnp.pad(field, ((0, 0), (1, 1), (0, 0)))
            field = advance(padded, speed_x, speed_y, inflow_row[:, None, None], inflow_indicator, boundary_wall_indicator)
        return field

    transported_integrals = lax.map(move_one, (droplet_integrals, flow_number_lengthwise, flow_number_crosswise, inflow_boundary_integrals))
    evaporated_quantity = evaporation_speed_stepwise[:, None, None, None] * thermal_factor[None, None] * transported_integrals
    gas_source = jnp.sum(evaporated_quantity, axis=0)
    remaining = transported_integrals - evaporated_quantity
    spray = couple(remaining, collision_coefficient, collision_target_share)
    return spray, gas_source
```

```python
import jax
import jax.numpy as jnp
from jax import lax
from jax.sharding import PartitionSpec as P

SUB = 4


def halo_rows(cells, width, outside):
    count = lax.axis_size("space")
    ends = count - 1
    dim = cells.ndim - 2
    head = lax.slice_in_dim(cells, 0, width, axis=dim)
    tail = lax.slice_in_dim(cells, cells.shape[dim] - width, cells.shape[dim], axis=dim)
    if outside:
        head, tail = 1 - head, 1 - tail
    west = lax.ppermute(tail, "space", [(i, i + 1) for i in range(ends)])
    east = lax.ppermute(head, "space", [(i + 1, i) for i in range(ends)])
    if outside:
        west, east = 1 - west, 1 - east
    return jnp.concatenate([west, cells, east], axis=dim)


def advance(field, speed_x, speed_y, inflow_value, inflow_rows, wall_rows):
    edge = jnp.zeros_like(field[..., :1, :])
    western = jnp.concatenate([edge, field[..., :-1, :]], axis=-2)
    eastern = jnp.concatenate([field[..., 1:, :], edge], axis=-2)
    border = jnp.zeros_like(field[..., :1])
    southern = jnp.concatenate([border, field[..., :-1]], axis=-1)
    northern = jnp.concatenate([field[..., 1:], border], axis=-1)
    moved = (
        field
        - jnp.maximum(speed_x, 0.0) * (field - western)
        - jnp.minimum(speed_x, 0.0) * (eastern - field)
    )
    moved = (
        moved
        - jnp.maximum(speed_y, 0.0) * (field - southern)
        - jnp.minimum(speed_y, 0.0) * (northern - field)
    )
    moved = jnp.where(inflow_rows > 0, inflow_value, moved)
    return jnp.where(wall_rows > 0, jnp.zeros_like(moved), moved)


def couple(cell_block, collision_coefficient, collision_target_share):
    mass_part = cell_block[:, 0]
    merge_rate = jnp.einsum(
        "sj,jxy->sxy", collision_coefficient, mass_part, precision=lax.Precision.HIGHEST
    )
    flux_terms = cell_block * merge_rate[:, None]
    gained = jnp.einsum(
        "sj,jmxy->smxy", collision_target_share, flux_terms, precision=lax.Precision.HIGHEST
    )
    return cell_block - flux_terms + gained


def shards(
    droplet_integrals,
    flow_number_lengthwise,
    flow_number_crosswise,
    inflow_boundary_integrals,
    boundary_wall_indicator,
    inflow_indicator,
    collision_coefficient,
    collision_target_share,
    evaporation_speed_stepwise,
    thermal_factor,
):
    groups = lax.axis_size("sec")
    group_size, moments, rows, columns = droplet_integrals.shape
    speed_x = flow_number_lengthwise[:, None, None, None]
    speed_y = flow_number_crosswise[:, None, None, None]
    inflow_value = inflow_boundary_integrals[:, :, None, None]
    field = halo_rows(droplet_integrals, SUB, False)
    wall_rows = halo_rows(boundary_wall_indicator, SUB, True)
    inflow_rows = halo_rows(inflow_indicator, SUB, False)
    for substep in range(SUB):
        field = advance(field, speed_x, speed_y, inflow_value, inflow_rows, wall_rows)
    moved = field[:, :, SUB : SUB + rows]
    block = columns // groups
    outgoing = jnp.transpose(
        moved.reshape(group_size, moments, rows, groups, block), (3, 0, 1, 2, 4)
    )
    arrived = lax.all_to_all(outgoing, "sec", split_axis=0, concat_axis=0, tiled=True)
    cell_block = arrived.reshape(groups * group_size, moments, rows, block)
    evaporated_quantity = (
        evaporation_speed_stepwise[:, None, None, None] * thermal_factor[None, None] * cell_block
    )
    gas_source = jnp.sum(evaporated_quantity, axis=0)
    remaining = cell_block - evaporated_quantity
    spray = couple(remaining, collision_coefficient, collision_target_share)
    return (spray, gas_source)


def solution(mesh):
    return jax.shard_map(
        shards,
        mesh=mesh,
        in_specs=(
            P("sec", None, "space", None),
            P("sec"),
            P("sec"),
            P("sec", None),
            P("space", None),
            P("space", None),
            P(),
            P(),
            P(),
            P("space", "sec"),
        ),
        out_specs=(P(None, None, "space", "sec"), P(None, "space", "sec")),
        check_vma=False,
    )
```

```python
import functools

import jax
import jax.numpy as jnp
from jax import lax
from jax.experimental import pallas as pl
from jax.experimental.pallas import tpu as pltpu
from jax.sharding import PartitionSpec as P

SUB = 4
CHUNK = 4


def halo_rows(cells, width, outside):
    count = lax.axis_size("space")
    ends = count - 1
    dim = cells.ndim - 2
    head = lax.slice_in_dim(cells, 0, width, axis=dim)
    tail = lax.slice_in_dim(cells, cells.shape[dim] - width, cells.shape[dim], axis=dim)
    if outside:
        head, tail = 1 - head, 1 - tail
    west = lax.ppermute(tail, "space", [(i, i + 1) for i in range(ends)])
    east = lax.ppermute(head, "space", [(i + 1, i) for i in range(ends)])
    if outside:
        west, east = 1 - west, 1 - east
    return jnp.concatenate([cells, east, west], axis=dim)


def transport_kernel(
    groups, ux_ref, uy_ref, iv_ref, field_hbm, wall_ref, infl_ref, out_hbm,
    buf, slots, in_sems, send_sems, recv_sems, local_sem,
):
    group_size, moments, span, columns = field_hbm.shape
    rows = span - 2 * SUB
    block = columns // groups
    chunks = group_size // CHUNK
    me = lax.axis_index("sec")
    row = lax.axis_index("space")

    loads = []
    for c in range(chunks):
        load = pltpu.make_async_copy(
            field_hbm.at[pl.ds(c * CHUNK, CHUNK)], buf.at[pl.ds(c * CHUNK, CHUNK)], in_sems.at[c]
        )
        load.start()
        loads.append(load)

    barrier = pltpu.get_barrier_semaphore()
    for d in range(1, groups):
        pl.semaphore_signal(
            barrier, 1, device_id=(lax.rem(me + d, groups), row),
            device_id_type=pl.DeviceIdType.MESH,
        )
    pl.semaphore_wait(barrier, groups - 1)

    def cols_of(k):
        return pl.ds(pl.multiple_of(k * block, block), block)

    for c in range(chunks):
        loads[c].wait()

        def body(i, carry):
            s = c * CHUNK + i
            ux = ux_ref[s]
            uy = uy_ref[s]
            px = jnp.maximum(ux, 0.0)
            nx = jnp.minimum(ux, 0.0)
            py = jnp.maximum(uy, 0.0)
            ny = jnp.minimum(uy, 0.0)
            for m in range(moments):
                q = buf[s, m]
                iv = iv_ref[s * moments + m]
                for step in range(SUB):
                    col = lax.broadcasted_iota(jnp.int32, q.shape, 1)
                    west = pltpu.roll(q, 1, 0)
                    east = pltpu.roll(q, span - 1, 0)
                    south = jnp.where(col == 0, 0.0, pltpu.roll(q, 1, 1))
                    north = jnp.where(col == columns - 1, 0.0, pltpu.roll(q, columns - 1, 1))
                    t = q - px * (q - west) - nx * (east - q)
                    t = t - py * (q - south) - ny * (north - q)
                    t = jnp.where(infl_ref[...] > 0, iv, t)
                    q = jnp.where(wall_ref[...] > 0, 0.0, t)
                slots[s, m] = q[:rows]
            return carry

        lax.fori_loop(0, CHUNK, body, 0)

        part = pl.ds(c * CHUNK, CHUNK)
        for d in range(1, groups):
            k = lax.rem(me + d, groups)
            pltpu.make_async_remote_copy(
                src_ref=slots.at[part, :, :, cols_of(k)],
                dst_ref=out_hbm.at[pl.ds(me * group_size + c * CHUNK, CHUNK)],
                send_sem=send_sems.at[d - 1],
                recv_sem=recv_sems.at[d - 1],
                device_id=(k, row),
                device_id_type=pl.DeviceIdType.MESH,
            ).start()
        pltpu.make_async_copy(
            slots.at[part, :, :, cols_of(me)],
            out_hbm.at[pl.ds(me * group_size + c * CHUNK, CHUNK)],
            local_sem,
        ).start()

    pltpu.make_async_copy(
        slots.at[:, :, :, cols_of(me)], out_hbm.at[pl.ds(me * group_size, group_size)], local_sem
    ).wait()
    for d in range(1, groups):
        k = lax.rem(me + d, groups)
        source = lax.rem(me + groups - d, groups)
        pltpu.make_async_remote_copy(
            src_ref=slots.at[:, :, :, cols_of(k)],
            dst_ref=out_hbm.at[pl.ds(me * group_size, group_size)],
            send_sem=send_sems.at[d - 1],
            recv_sem=recv_sems.at[d - 1],
            device_id=(k, row),
            device_id_type=pl.DeviceIdType.MESH,
        ).wait_send()
        pltpu.make_async_remote_copy(
            src_ref=slots.at[:, :, :, cols_of(k)],
            dst_ref=out_hbm.at[pl.ds(source * group_size, group_size)],
            send_sem=send_sems.at[d - 1],
            recv_sem=recv_sems.at[d - 1],
            device_id=(k, row),
            device_id_type=pl.DeviceIdType.MESH,
        ).wait_recv()


def transport_exchange(speed_x, speed_y, inflow_value, field, wall_rows, inflow_rows):
    groups = lax.axis_size("sec")
    group_size, moments, span, columns = field.shape
    rows = span - 2 * SUB
    block = columns // groups
    smem = pl.BlockSpec(memory_space=pltpu.SMEM)
    vmem = pl.BlockSpec(memory_space=pltpu.VMEM)
    anywhere = pl.BlockSpec(memory_space=pl.ANY)
    flops = 30 * SUB * field.size
    return pl.pallas_call(
        functools.partial(transport_kernel, groups),
        out_shape=jax.ShapeDtypeStruct((groups * group_size, moments, rows, block), jnp.float32),
        in_specs=[smem, smem, smem, anywhere, vmem, vmem],
        out_specs=anywhere,
        scratch_shapes=[
            pltpu.VMEM((group_size, moments, span, columns), jnp.float32),
            pltpu.VMEM((group_size, moments, rows, columns), jnp.float32),
            pltpu.SemaphoreType.DMA((group_size // CHUNK,)),
            pltpu.SemaphoreType.DMA((groups - 1,)),
            pltpu.SemaphoreType.DMA((groups - 1,)),
            pltpu.SemaphoreType.DMA(()),
        ],
        compiler_params=pltpu.CompilerParams(
            collective_id=0, has_side_effects=True, vmem_limit_bytes=60 * 1024 * 1024
        ),
        cost_estimate=pl.CostEstimate(
            flops=flops, bytes_accessed=4 * (field.size * 2), transcendentals=0
        ),
    )(speed_x, speed_y, inflow_value.reshape(-1), field, wall_rows, inflow_rows)


def couple(cell_block, collision_coefficient, collision_target_share):
    mass_part = cell_block[:, 0]
    merge_rate = jnp.einsum(
        "sj,jxy->sxy", collision_coefficient, mass_part, precision=lax.Precision.HIGHEST
    )
    flux_terms = cell_block * merge_rate[:, None]
    gained = jnp.einsum(
        "sj,jmxy->smxy", collision_target_share, flux_terms, precision=lax.Precision.HIGHEST
    )
    return cell_block - flux_terms + gained


def shards(
    droplet_integrals,
    flow_number_lengthwise,
    flow_number_crosswise,
    inflow_boundary_integrals,
    boundary_wall_indicator,
    inflow_indicator,
    collision_coefficient,
    collision_target_share,
    evaporation_speed_stepwise,
    thermal_factor,
):
    field = halo_rows(droplet_integrals, SUB, False)
    wall_rows = halo_rows(boundary_wall_indicator, SUB, True)
    inflow_rows = halo_rows(inflow_indicator, SUB, False)
    cell_block = transport_exchange(
        flow_number_lengthwise, flow_number_crosswise, inflow_boundary_integrals,
        field, wall_rows, inflow_rows,
    )
    evaporated_quantity = (
        evaporation_speed_stepwise[:, None, None, None] * thermal_factor[None, None] * cell_block
    )
    gas_source = jnp.sum(evaporated_quantity, axis=0)
    remaining = cell_block - evaporated_quantity
    spray = couple(remaining, collision_coefficient, collision_target_share)
    return (spray, gas_source)


def solution(mesh):
    return jax.shard_map(
        shards,
        mesh=mesh,
        in_specs=(
            P("sec", None, "space", None),
            P("sec"),
            P("sec"),
            P("sec", None),
            P("space", None),
            P("space", None),
            P(),
            P(),
            P(),
            P("space", "sec"),
        ),
        out_specs=(P(None, None, "space", "sec"), P(None, "space", "sec")),
        check_vma=False,
    )
```

```python
import functools

import jax
import jax.numpy as jnp
from jax import lax
from jax.experimental import pallas as pl
from jax.experimental.pallas import tpu as pltpu
from jax.sharding import PartitionSpec as P

SUB = 4
CHUNK = 4
MESH = pl.DeviceIdType.MESH


def transport_kernel(
    groups, lines,
    ux_ref, uy_ref, iv_ref, field_hbm, wall_ref, infl_ref,
    out_hbm,
    local, halo, wall_halo, infl_halo, slots,
    load_sems, halo_recv, halo_send, mask_recv, mask_send, send_sems, recv_sems, local_sem,
):
    group_size, moments, rows, columns = field_hbm.shape
    span = 2 * rows
    block = columns // groups
    chunks = group_size // CHUNK
    me = lax.axis_index("sec")
    row = lax.axis_index("space")
    has_west = (row + lines - 1) // lines
    has_east = 1 - row // (lines - 1)
    west = (me, row - 1)
    east = (me, row + 1)
    first = pl.ds(0, SUB)
    last = pl.ds(SUB, SUB)

    loads = []
    for c in range(chunks):
        part = pl.ds(c * CHUNK, CHUNK)
        load = pltpu.make_async_copy(field_hbm.at[part], local.at[part], load_sems.at[c])
        load.start()
        loads.append(load)

    @pl.when(row == 0)
    def _():
        halo[:, :, last, :] = jnp.zeros((group_size, moments, SUB, columns), jnp.float32)
        wall_halo[last, :] = jnp.ones((SUB, columns), jnp.int32)
        infl_halo[last, :] = jnp.zeros((SUB, columns), jnp.int32)

    @pl.when(row == lines - 1)
    def _():
        halo[:, :, first, :] = jnp.zeros((group_size, moments, SUB, columns), jnp.float32)
        wall_halo[first, :] = jnp.ones((SUB, columns), jnp.int32)
        infl_halo[first, :] = jnp.zeros((SUB, columns), jnp.int32)

    barrier = pltpu.get_barrier_semaphore()
    for d in range(1, groups):
        pl.semaphore_signal(barrier, 1, device_id=(lax.rem(me + d, groups), row), device_id_type=MESH)

    @pl.when(row > 0)
    def _():
        pl.semaphore_signal(barrier, 1, device_id=west, device_id_type=MESH)

    @pl.when(row < lines - 1)
    def _():
        pl.semaphore_signal(barrier, 1, device_id=east, device_id_type=MESH)

    pl.semaphore_wait(barrier, groups - 1 + has_west + has_east)

    def halo_copy(src, dst, direction, sem_recv, sem_send):
        return pltpu.make_async_remote_copy(
            src_ref=src, dst_ref=dst, send_sem=sem_send, recv_sem=sem_recv,
            device_id=west if direction == 0 else east, device_id_type=MESH,
        )

    def field_halo(c, direction):
        part = pl.ds(c * CHUNK, CHUNK)
        if direction == 0:
            return halo_copy(field_hbm.at[part, :, first, :], halo.at[part, :, first, :], 0,
                             halo_recv.at[0, c], halo_send.at[0])
        return halo_copy(field_hbm.at[part, :, pl.ds(rows - SUB, SUB), :], halo.at[part, :, last, :], 1,
                         halo_recv.at[1, c], halo_send.at[1])

    def mask_halo(ref, store, k, direction):
        if direction == 0:
            return halo_copy(ref.at[first, :], store.at[first, :], 0, mask_recv.at[k, 0], mask_send.at[k, 0])
        return halo_copy(ref.at[pl.ds(rows - SUB, SUB), :], store.at[last, :], 1,
                         mask_recv.at[k, 1], mask_send.at[k, 1])

    @pl.when(row > 0)
    def _():
        mask_halo(wall_ref, wall_halo, 0, 0).start()
        mask_halo(infl_ref, infl_halo, 1, 0).start()
        for c in range(chunks):
            field_halo(c, 0).start()

    @pl.when(row < lines - 1)
    def _():
        mask_halo(wall_ref, wall_halo, 0, 1).start()
        mask_halo(infl_ref, infl_halo, 1, 1).start()
        for c in range(chunks):
            field_halo(c, 1).start()

    @pl.when(row < lines - 1)
    def _():
        mask_halo(wall_ref, wall_halo, 0, 0).wait_recv()
        mask_halo(infl_ref, infl_halo, 1, 0).wait_recv()

    @pl.when(row > 0)
    def _():
        mask_halo(wall_ref, wall_halo, 0, 1).wait_recv()
        mask_halo(infl_ref, infl_halo, 1, 1).wait_recv()

    def cols_of(k):
        return pl.ds(pl.multiple_of(k * block, block), block)

    for c in range(chunks):
        loads[c].wait()

        @pl.when(row < lines - 1)
        def _():
            field_halo(c, 0).wait_recv()

        @pl.when(row > 0)
        def _():
            field_halo(c, 1).wait_recv()

        def body(i, carry):
            s = c * CHUNK + i
            ux = ux_ref[s]
            uy = uy_ref[s]
            px = jnp.maximum(ux, 0.0)
            nx = jnp.minimum(ux, 0.0)
            py = jnp.maximum(uy, 0.0)
            ny = jnp.minimum(uy, 0.0)
            for m in range(moments):
                q = jnp.concatenate([local[s, m], halo[s, m]], axis=0)
                iv = iv_ref[s * moments + m]
                for step in range(SUB):
                    col = lax.broadcasted_iota(jnp.int32, q.shape, 1)
                    western = pltpu.roll(q, 1, 0)
                    eastern = pltpu.roll(q, span - 1, 0)
                    southern = jnp.where(col == 0, 0.0, pltpu.roll(q, 1, 1))
                    northern = jnp.where(col == columns - 1, 0.0, pltpu.roll(q, columns - 1, 1))
                    t = q - px * (q - western) - nx * (eastern - q)
                    t = t - py * (q - southern) - ny * (northern - q)
                    inflow_rows = jnp.concatenate([infl_ref[...], infl_halo[...]], axis=0)
                    wall_rows = jnp.concatenate([wall_ref[...], wall_halo[...]], axis=0)
                    t = jnp.where(inflow_rows > 0, iv, t)
                    q = jnp.where(wall_rows > 0, 0.0, t)
                slots[s, m] = q[:rows]
            return carry

        lax.fori_loop(0, CHUNK, body, 0)

        part = pl.ds(c * CHUNK, CHUNK)
        for d in range(1, groups):
            k = lax.rem(me + d, groups)
            pltpu.make_async_remote_copy(
                src_ref=slots.at[part, :, :, cols_of(k)],
                dst_ref=out_hbm.at[pl.ds(me * group_size + c * CHUNK, CHUNK)],
                send_sem=send_sems.at[d - 1],
                recv_sem=recv_sems.at[d - 1],
                device_id=(k, row),
                device_id_type=MESH,
            ).start()
        pltpu.make_async_copy(
            slots.at[part, :, :, cols_of(me)],
            out_hbm.at[pl.ds(me * group_size + c * CHUNK, CHUNK)],
            local_sem,
        ).start()

    @pl.when(row > 0)
    def _():
        mask_halo(wall_ref, wall_halo, 0, 0).wait_send()
        mask_halo(infl_ref, infl_halo, 1, 0).wait_send()
        halo_copy(field_hbm.at[:, :, first, :], halo.at[:, :, first, :], 0,
                  halo_recv.at[0, 0], halo_send.at[0]).wait_send()

    @pl.when(row < lines - 1)
    def _():
        mask_halo(wall_ref, wall_halo, 0, 1).wait_send()
        mask_halo(infl_ref, infl_halo, 1, 1).wait_send()
        halo_copy(field_hbm.at[:, :, pl.ds(rows - SUB, SUB), :], halo.at[:, :, last, :], 1,
                  halo_recv.at[1, 0], halo_send.at[1]).wait_send()

    pltpu.make_async_copy(
        slots.at[:, :, :, cols_of(me)], out_hbm.at[pl.ds(me * group_size, group_size)], local_sem
    ).wait()
    for d in range(1, groups):
        k = lax.rem(me + d, groups)
        source = lax.rem(me + groups - d, groups)
        pltpu.make_async_remote_copy(
            src_ref=slots.at[:, :, :, cols_of(k)],
            dst_ref=out_hbm.at[pl.ds(me * group_size, group_size)],
            send_sem=send_sems.at[d - 1],
            recv_sem=recv_sems.at[d - 1],
            device_id=(k, row),
            device_id_type=MESH,
        ).wait_send()
        pltpu.make_async_remote_copy(
            src_ref=slots.at[:, :, :, cols_of(k)],
            dst_ref=out_hbm.at[pl.ds(source * group_size, group_size)],
            send_sem=send_sems.at[d - 1],
            recv_sem=recv_sems.at[d - 1],
            device_id=(k, row),
            device_id_type=MESH,
        ).wait_recv()


def transport_exchange(speed_x, speed_y, inflow_value, field, wall_rows, inflow_rows):
    groups = lax.axis_size("sec")
    lines = lax.axis_size("space")
    group_size, moments, rows, columns = field.shape
    block = columns // groups
    chunks = group_size // CHUNK
    smem = pl.BlockSpec(memory_space=pltpu.SMEM)
    vmem = pl.BlockSpec(memory_space=pltpu.VMEM)
    anywhere = pl.BlockSpec(memory_space=pl.ANY)
    flops = 60 * SUB * field.size
    return pl.pallas_call(
        functools.partial(transport_kernel, groups, lines),
        out_shape=jax.ShapeDtypeStruct((groups * group_size, moments, rows, block), jnp.float32),
        in_specs=[smem, smem, smem, anywhere, vmem, vmem],
        out_specs=anywhere,
        scratch_shapes=[
            pltpu.VMEM((group_size, moments, rows, columns), jnp.float32),
            pltpu.VMEM((group_size, moments, rows, columns), jnp.float32),
            pltpu.VMEM((rows, columns), jnp.int32),
            pltpu.VMEM((rows, columns), jnp.int32),
            pltpu.VMEM((group_size, moments, rows, columns), jnp.float32),
            pltpu.SemaphoreType.DMA((chunks,)),
            pltpu.SemaphoreType.DMA((2, chunks)),
            pltpu.SemaphoreType.DMA((2,)),
            pltpu.SemaphoreType.DMA((2, 2)),
            pltpu.SemaphoreType.DMA((2, 2)),
            pltpu.SemaphoreType.DMA((groups - 1,)),
            pltpu.SemaphoreType.DMA((groups - 1,)),
            pltpu.SemaphoreType.DMA(()),
        ],
        compiler_params=pltpu.CompilerParams(
            collective_id=0, has_side_effects=True, vmem_limit_bytes=60 * 1024 * 1024
        ),
        cost_estimate=pl.CostEstimate(
            flops=flops, bytes_accessed=4 * (field.size * 2), transcendentals=0
        ),
    )(speed_x, speed_y, inflow_value.reshape(-1), field, wall_rows, inflow_rows)


def couple(cell_block, collision_coefficient, collision_target_share):
    mass_part = cell_block[:, 0]
    merge_rate = jnp.einsum(
        "sj,jxy->sxy", collision_coefficient, mass_part, precision=lax.Precision.HIGHEST
    )
    flux_terms = cell_block * merge_rate[:, None]
    gained = jnp.einsum(
        "sj,jmxy->smxy", collision_target_share, flux_terms, precision=lax.Precision.HIGHEST
    )
    return cell_block - flux_terms + gained


def shards(
    droplet_integrals,
    flow_number_lengthwise,
    flow_number_crosswise,
    inflow_boundary_integrals,
    boundary_wall_indicator,
    inflow_indicator,
    collision_coefficient,
    collision_target_share,
    evaporation_speed_stepwise,
    thermal_factor,
):
    cell_block = transport_exchange(
        flow_number_lengthwise, flow_number_crosswise, inflow_boundary_integrals,
        droplet_integrals, boundary_wall_indicator, inflow_indicator,
    )
    evaporated_quantity = (
        evaporation_speed_stepwise[:, None, None, None] * thermal_factor[None, None] * cell_block
    )
    gas_source = jnp.sum(evaporated_quantity, axis=0)
    remaining = cell_block - evaporated_quantity
    spray = couple(remaining, collision_coefficient, collision_target_share)
    return (spray, gas_source)


def solution(mesh):
    return jax.shard_map(
        shards,
        mesh=mesh,
        in_specs=(
            P("sec", None, "space", None),
            P("sec"),
            P("sec"),
            P("sec", None),
            P("space", None),
            P("space", None),
            P(),
            P(),
            P(),
            P("space", "sec"),
        ),
        out_specs=(P(None, None, "space", "sec"), P(None, "space", "sec")),
        check_vma=False,
    )
```

```python
import functools

import jax
import jax.numpy as jnp
from jax import lax
from jax.experimental import pallas as pl
from jax.experimental.pallas import tpu as pltpu
from jax.sharding import PartitionSpec as P

SUB = 4
CHUNK = 4
MESH = pl.DeviceIdType.MESH


def transport_kernel(
    groups, lines,
    ux_ref, uy_ref, iv_ref, field_hbm, wall_ref, infl_ref,
    out_hbm,
    local, halo, wall_halo, infl_halo, slots,
    load_sems, halo_recv, halo_send, mask_recv, mask_send, send_sems, recv_sems, local_sem,
):
    group_size, moments, rows, columns = field_hbm.shape
    span = 2 * rows
    block = columns // groups
    chunks = group_size // CHUNK
    me = lax.axis_index("sec")
    row = lax.axis_index("space")
    has_west = (row + lines - 1) // lines
    has_east = 1 - row // (lines - 1)
    west = (me, row - 1)
    east = (me, row + 1)
    first = pl.ds(0, SUB)
    last = pl.ds(SUB, SUB)

    loads = []
    for c in range(chunks):
        part = pl.ds(c * CHUNK, CHUNK)
        load = pltpu.make_async_copy(field_hbm.at[part], local.at[part], load_sems.at[c])
        load.start()
        loads.append(load)

    @pl.when(row == 0)
    def _():
        halo[:, :, last, :] = jnp.zeros((group_size, moments, SUB, columns), jnp.float32)
        wall_halo[last, :] = jnp.ones((SUB, columns), jnp.int32)
        infl_halo[last, :] = jnp.zeros((SUB, columns), jnp.int32)

    @pl.when(row == lines - 1)
    def _():
        halo[:, :, first, :] = jnp.zeros((group_size, moments, SUB, columns), jnp.float32)
        wall_halo[first, :] = jnp.ones((SUB, columns), jnp.int32)
        infl_halo[first, :] = jnp.zeros((SUB, columns), jnp.int32)

    barrier = pltpu.get_barrier_semaphore()
    for d in range(1, groups):
        pl.semaphore_signal(barrier, 1, device_id=(lax.rem(me + d, groups), row), device_id_type=MESH)

    @pl.when(row > 0)
    def _():
        pl.semaphore_signal(barrier, 1, device_id=west, device_id_type=MESH)

    @pl.when(row < lines - 1)
    def _():
        pl.semaphore_signal(barrier, 1, device_id=east, device_id_type=MESH)

    pl.semaphore_wait(barrier, groups - 1 + has_west + has_east)

    def halo_copy(src, dst, direction, sem_recv, sem_send):
        return pltpu.make_async_remote_copy(
            src_ref=src, dst_ref=dst, send_sem=sem_send, recv_sem=sem_recv,
            device_id=west if direction == 0 else east, device_id_type=MESH,
        )

    def field_halo(c, direction):
        part = pl.ds(c * CHUNK, CHUNK)
        if direction == 0:
            return halo_copy(field_hbm.at[part, :, first, :], halo.at[part, :, first, :], 0,
                             halo_recv.at[0, c], halo_send.at[0])
        return halo_copy(field_hbm.at[part, :, pl.ds(rows - SUB, SUB), :], halo.at[part, :, last, :], 1,
                         halo_recv.at[1, c], halo_send.at[1])

    def mask_halo(ref, store, k, direction):
        if direction == 0:
            return halo_copy(ref.at[first, :], store.at[first, :], 0, mask_recv.at[k, 0], mask_send.at[k, 0])
        return halo_copy(ref.at[pl.ds(rows - SUB, SUB), :], store.at[last, :], 1,
                         mask_recv.at[k, 1], mask_send.at[k, 1])

    @pl.when(row > 0)
    def _():
        mask_halo(wall_ref, wall_halo, 0, 0).start()
        mask_halo(infl_ref, infl_halo, 1, 0).start()
        for c in range(chunks):
            field_halo(c, 0).start()

    @pl.when(row < lines - 1)
    def _():
        mask_halo(wall_ref, wall_halo, 0, 1).start()
        mask_halo(infl_ref, infl_halo, 1, 1).start()
        for c in range(chunks):
            field_halo(c, 1).start()

    @pl.when(row < lines - 1)
    def _():
        mask_halo(wall_ref, wall_halo, 0, 0).wait_recv()
        mask_halo(infl_ref, infl_halo, 1, 0).wait_recv()

    @pl.when(row > 0)
    def _():
        mask_halo(wall_ref, wall_halo, 0, 1).wait_recv()
        mask_halo(infl_ref, infl_halo, 1, 1).wait_recv()

    def cols_of(k):
        return pl.ds(pl.multiple_of(k * block, block), block)

    for c in range(chunks):
        loads[c].wait()

        @pl.when(row < lines - 1)
        def _():
            field_halo(c, 0).wait_recv()

        @pl.when(row > 0)
        def _():
            field_halo(c, 1).wait_recv()

        def body(i, carry):
            s = c * CHUNK + i
            ux = ux_ref[s]
            uy = uy_ref[s]
            px = jnp.maximum(ux, 0.0)
            nx = jnp.minimum(ux, 0.0)
            py = jnp.maximum(uy, 0.0)
            ny = jnp.minimum(uy, 0.0)
            for m in range(moments):
                q = jnp.concatenate([local[s, m], halo[s, m]], axis=0)
                iv = iv_ref[s * moments + m]
                for step in range(SUB):
                    col = lax.broadcasted_iota(jnp.int32, q.shape, 1)
                    western = pltpu.roll(q, 1, 0)
                    eastern = pltpu.roll(q, span - 1, 0)
                    southern = jnp.where(col == 0, 0.0, pltpu.roll(q, 1, 1))
                    northern = jnp.where(col == columns - 1, 0.0, pltpu.roll(q, columns - 1, 1))
                    t = q - px * (q - western) - nx * (eastern - q)
                    t = t - py * (q - southern) - ny * (northern - q)
                    inflow_rows = jnp.concatenate([infl_ref[...], infl_halo[...]], axis=0)
                    wall_rows = jnp.concatenate([wall_ref[...], wall_halo[...]], axis=0)
                    t = jnp.where(inflow_rows > 0, iv, t)
                    q = jnp.where(wall_rows > 0, 0.0, t)
                slots[s, m] = q[:rows]
            return carry

        lax.fori_loop(0, CHUNK, body, 0)

        part = pl.ds(c * CHUNK, CHUNK)
        for d in range(1, groups):
            k = lax.rem(me + d, groups)
            pltpu.make_async_remote_copy(
                src_ref=slots.at[part, :, :, cols_of(k)],
                dst_ref=out_hbm.at[pl.ds(me * group_size + c * CHUNK, CHUNK)],
                send_sem=send_sems.at[d - 1],
                recv_sem=recv_sems.at[d - 1],
                device_id=(k, row),
                device_id_type=MESH,
            ).start()
        pltpu.make_async_copy(
            slots.at[part, :, :, cols_of(me)],
            out_hbm.at[pl.ds(me * group_size + c * CHUNK, CHUNK)],
            local_sem,
        ).start()

    @pl.when(row > 0)
    def _():
        mask_halo(wall_ref, wall_halo, 0, 0).wait_send()
        mask_halo(infl_ref, infl_halo, 1, 0).wait_send()
        halo_copy(field_hbm.at[:, :, first, :], halo.at[:, :, first, :], 0,
                  halo_recv.at[0, 0], halo_send.at[0]).wait_send()

    @pl.when(row < lines - 1)
    def _():
        mask_halo(wall_ref, wall_halo, 0, 1).wait_send()
        mask_halo(infl_ref, infl_halo, 1, 1).wait_send()
        halo_copy(field_hbm.at[:, :, pl.ds(rows - SUB, SUB), :], halo.at[:, :, last, :], 1,
                  halo_recv.at[1, 0], halo_send.at[1]).wait_send()

    pltpu.make_async_copy(
        slots.at[:, :, :, cols_of(me)], out_hbm.at[pl.ds(me * group_size, group_size)], local_sem
    ).wait()
    for d in range(1, groups):
        k = lax.rem(me + d, groups)
        source = lax.rem(me + groups - d, groups)
        pltpu.make_async_remote_copy(
            src_ref=slots.at[:, :, :, cols_of(k)],
            dst_ref=out_hbm.at[pl.ds(me * group_size, group_size)],
            send_sem=send_sems.at[d - 1],
            recv_sem=recv_sems.at[d - 1],
            device_id=(k, row),
            device_id_type=MESH,
        ).wait_send()
        pltpu.make_async_remote_copy(
            src_ref=slots.at[:, :, :, cols_of(k)],
            dst_ref=out_hbm.at[pl.ds(source * group_size, group_size)],
            send_sem=send_sems.at[d - 1],
            recv_sem=recv_sems.at[d - 1],
            device_id=(k, row),
            device_id_type=MESH,
        ).wait_recv()


def transport_exchange(speed_x, speed_y, inflow_value, field, wall_rows, inflow_rows):
    groups = lax.axis_size("sec")
    lines = lax.axis_size("space")
    group_size, moments, rows, columns = field.shape
    block = columns // groups
    chunks = group_size // CHUNK
    smem = pl.BlockSpec(memory_space=pltpu.SMEM)
    vmem = pl.BlockSpec(memory_space=pltpu.VMEM)
    anywhere = pl.BlockSpec(memory_space=pl.ANY)
    flops = 60 * SUB * field.size
    return pl.pallas_call(
        functools.partial(transport_kernel, groups, lines),
        out_shape=jax.ShapeDtypeStruct((groups * group_size, moments, rows, block), jnp.float32),
        in_specs=[smem, smem, smem, anywhere, vmem, vmem],
        out_specs=anywhere,
        scratch_shapes=[
            pltpu.VMEM((group_size, moments, rows, columns), jnp.float32),
            pltpu.VMEM((group_size, moments, rows, columns), jnp.float32),
            pltpu.VMEM((rows, columns), jnp.int32),
            pltpu.VMEM((rows, columns), jnp.int32),
            pltpu.VMEM((group_size, moments, rows, columns), jnp.float32),
            pltpu.SemaphoreType.DMA((chunks,)),
            pltpu.SemaphoreType.DMA((2, chunks)),
            pltpu.SemaphoreType.DMA((2,)),
            pltpu.SemaphoreType.DMA((2, 2)),
            pltpu.SemaphoreType.DMA((2, 2)),
            pltpu.SemaphoreType.DMA((groups - 1,)),
            pltpu.SemaphoreType.DMA((groups - 1,)),
            pltpu.SemaphoreType.DMA(()),
        ],
        compiler_params=pltpu.CompilerParams(
            collective_id=0, has_side_effects=True, vmem_limit_bytes=60 * 1024 * 1024
        ),
        cost_estimate=pl.CostEstimate(
            flops=flops, bytes_accessed=4 * (field.size * 2), transcendentals=0
        ),
    )(speed_x, speed_y, inflow_value.reshape(-1), field, wall_rows, inflow_rows)


def post_kernel(rate_ref, tf_ref, coef_ref, share_ref, x_ref, spray_ref, gas_ref):
    span, _ = gas_ref.shape
    rows = tf_ref.shape[0]
    moments = span // rows
    sections = rate_ref.shape[0]
    highest = lax.Precision.HIGHEST
    rate = rate_ref[...]
    coef = coef_ref[...]
    share = share_ref[...]
    for r in range(rows):
        factor = rate * tf_ref[pl.ds(r, 1), :]
        remaining = []
        for m in range(moments):
            x = x_ref[pl.ds(m * rows + r, sections, stride=span), :]
            evaporated = factor * x
            gas_ref[pl.ds(m * rows + r, 1), :] = jnp.sum(evaporated, axis=0, keepdims=True)
            remaining.append(x - evaporated)
        merge_rate = jnp.dot(coef, remaining[0], precision=highest, preferred_element_type=jnp.float32)
        for m in range(moments):
            flux = remaining[m] * merge_rate
            gained = jnp.dot(share, flux, precision=highest, preferred_element_type=jnp.float32)
            spray_ref[pl.ds(m * rows + r, sections, stride=span), :] = remaining[m] - flux + gained


def evaporate_couple(cell_block, rates, thermal_factor, coefficient, share):
    sections, moments, rows, block = cell_block.shape
    strip = 128
    span = moments * rows
    flat = cell_block.reshape(sections * span, block)
    full = lambda shape: pl.BlockSpec(shape, lambda i: (0, 0))
    spray, gas = pl.pallas_call(
        post_kernel,
        grid=(block // strip,),
        in_specs=[
            full((sections, 1)),
            pl.BlockSpec((rows, strip), lambda i: (0, i)),
            full((sections, sections)),
            full((sections, sections)),
            pl.BlockSpec((sections * span, strip), lambda i: (0, i)),
        ],
        out_specs=[
            pl.BlockSpec((sections * span, strip), lambda i: (0, i)),
            pl.BlockSpec((span, strip), lambda i: (0, i)),
        ],
        out_shape=[
            jax.ShapeDtypeStruct((sections * span, block), jnp.float32),
            jax.ShapeDtypeStruct((span, block), jnp.float32),
        ],
        cost_estimate=pl.CostEstimate(
            flops=2 * sections * sections * flat.size // sections * (moments + 1) // moments * 6,
            bytes_accessed=8 * flat.size, transcendentals=0,
        ),
    )(rates.reshape(sections, 1), thermal_factor, coefficient, share, flat)
    return spray.reshape(sections, moments, rows, block), gas.reshape(moments, rows, block)


def shards(
    droplet_integrals,
    flow_number_lengthwise,
    flow_number_crosswise,
    inflow_boundary_integrals,
    boundary_wall_indicator,
    inflow_indicator,
    collision_coefficient,
    collision_target_share,
    evaporation_speed_stepwise,
    thermal_factor,
):
    cell_block = transport_exchange(
        flow_number_lengthwise, flow_number_crosswise, inflow_boundary_integrals,
        droplet_integrals, boundary_wall_indicator, inflow_indicator,
    )
    spray, gas_source = evaporate_couple(
        cell_block, evaporation_speed_stepwise, thermal_factor,
        collision_coefficient, collision_target_share,
    )
    return (spray, gas_source)


def solution(mesh):
    return jax.shard_map(
        shards,
        mesh=mesh,
        in_specs=(
            P("sec", None, "space", None),
            P("sec"),
            P("sec"),
            P("sec", None),
            P("space", None),
            P("space", None),
            P(),
            P(),
            P(),
            P("space", "sec"),
        ),
        out_specs=(P(None, None, "space", "sec"), P(None, "space", "sec")),
        check_vma=False,
    )
```

```python
import functools

import jax
import jax.numpy as jnp
from jax import lax
from jax.experimental import pallas as pl
from jax.experimental.pallas import tpu as pltpu
from jax.sharding import PartitionSpec as P

SUB = 4
CHUNK = 4
MESH = pl.DeviceIdType.MESH


def transport_kernel(
    groups, lines,
    ux_ref, uy_ref, iv_ref, field_hbm, wall_ref, infl_ref,
    out_hbm,
    local, halo, wall_halo, infl_halo, slots,
    load_sems, halo_recv, halo_send, mask_recv, mask_send, send_sems, recv_sems, local_sem,
):
    group_size, moments, rows, columns = field_hbm.shape
    span = 2 * rows
    block = columns // groups
    chunks = group_size // CHUNK
    me = lax.axis_index("sec")
    row = lax.axis_index("space")
    has_west = (row + lines - 1) // lines
    has_east = 1 - row // (lines - 1)
    west = (me, row - 1)
    east = (me, row + 1)
    first = pl.ds(0, SUB)
    last = pl.ds(SUB, SUB)

    loads = []
    for c in range(chunks):
        part = pl.ds(c * CHUNK, CHUNK)
        load = pltpu.make_async_copy(field_hbm.at[part], local.at[part], load_sems.at[c])
        load.start()
        loads.append(load)

    @pl.when(row == 0)
    def _():
        halo[:, :, last, :] = jnp.zeros((group_size, moments, SUB, columns), jnp.float32)
        wall_halo[last, :] = jnp.ones((SUB, columns), jnp.int32)
        infl_halo[last, :] = jnp.zeros((SUB, columns), jnp.int32)

    @pl.when(row == lines - 1)
    def _():
        halo[:, :, first, :] = jnp.zeros((group_size, moments, SUB, columns), jnp.float32)
        wall_halo[first, :] = jnp.ones((SUB, columns), jnp.int32)
        infl_halo[first, :] = jnp.zeros((SUB, columns), jnp.int32)

    barrier = pltpu.get_barrier_semaphore()
    for d in range(1, groups):
        pl.semaphore_signal(barrier, 1, device_id=(lax.rem(me + d, groups), row), device_id_type=MESH)

    @pl.when(row > 0)
    def _():
        pl.semaphore_signal(barrier, 1, device_id=west, device_id_type=MESH)

    @pl.when(row < lines - 1)
    def _():
        pl.semaphore_signal(barrier, 1, device_id=east, device_id_type=MESH)

    pl.semaphore_wait(barrier, groups - 1 + has_west + has_east)

    def halo_copy(src, dst, direction, sem_recv, sem_send):
        return pltpu.make_async_remote_copy(
            src_ref=src, dst_ref=dst, send_sem=sem_send, recv_sem=sem_recv,
            device_id=west if direction == 0 else east, device_id_type=MESH,
        )

    def field_halo(c, direction):
        part = pl.ds(c * CHUNK, CHUNK)
        if direction == 0:
            return halo_copy(field_hbm.at[part, :, first, :], halo.at[part, :, first, :], 0,
                             halo_recv.at[0, c], halo_send.at[0])
        return halo_copy(field_hbm.at[part, :, pl.ds(rows - SUB, SUB), :], halo.at[part, :, last, :], 1,
                         halo_recv.at[1, c], halo_send.at[1])

    def mask_halo(ref, store, k, direction):
        if direction == 0:
            return halo_copy(ref.at[first, :], store.at[first, :], 0, mask_recv.at[k, 0], mask_send.at[k, 0])
        return halo_copy(ref.at[pl.ds(rows - SUB, SUB), :], store.at[last, :], 1,
                         mask_recv.at[k, 1], mask_send.at[k, 1])

    @pl.when(row > 0)
    def _():
        mask_halo(wall_ref, wall_halo, 0, 0).start()
        mask_halo(infl_ref, infl_halo, 1, 0).start()
        for c in range(chunks):
            field_halo(c, 0).start()

    @pl.when(row < lines - 1)
    def _():
        mask_halo(wall_ref, wall_halo, 0, 1).start()
        mask_halo(infl_ref, infl_halo, 1, 1).start()
        for c in range(chunks):
            field_halo(c, 1).start()

    @pl.when(row < lines - 1)
    def _():
        mask_halo(wall_ref, wall_halo, 0, 0).wait_recv()
        mask_halo(infl_ref, infl_halo, 1, 0).wait_recv()

    @pl.when(row > 0)
    def _():
        mask_halo(wall_ref, wall_halo, 0, 1).wait_recv()
        mask_halo(infl_ref, infl_halo, 1, 1).wait_recv()

    def cols_of(k):
        return pl.ds(pl.multiple_of(k * block, block), block)

    for c in range(chunks):
        loads[c].wait()

        @pl.when(row < lines - 1)
        def _():
            field_halo(c, 0).wait_recv()

        @pl.when(row > 0)
        def _():
            field_halo(c, 1).wait_recv()

        def body(i, carry):
            s = c * CHUNK + i
            ux = ux_ref[s]
            uy = uy_ref[s]
            px = jnp.maximum(ux, 0.0)
            nx = jnp.minimum(ux, 0.0)
            py = jnp.maximum(uy, 0.0)
            ny = jnp.minimum(uy, 0.0)
            for m in range(moments):
                q = jnp.concatenate([local[s, m], halo[s, m]], axis=0)
                iv = iv_ref[m, s]
                for step in range(SUB):
                    col = lax.broadcasted_iota(jnp.int32, q.shape, 1)
                    western = pltpu.roll(q, 1, 0)
                    eastern = pltpu.roll(q, span - 1, 0)
                    southern = jnp.where(col == 0, 0.0, pltpu.roll(q, 1, 1))
                    northern = jnp.where(col == columns - 1, 0.0, pltpu.roll(q, columns - 1, 1))
                    t = q - px * (q - western) - nx * (eastern - q)
                    t = t - py * (q - southern) - ny * (northern - q)
                    inflow_rows = jnp.concatenate([infl_ref[...], infl_halo[...]], axis=0)
                    wall_rows = jnp.concatenate([wall_ref[...], wall_halo[...]], axis=0)
                    t = jnp.where(inflow_rows > 0, iv, t)
                    q = jnp.where(wall_rows > 0, 0.0, t)
                slots[s, m] = q[:rows]
            return carry

        lax.fori_loop(0, CHUNK, body, 0)

        part = pl.ds(c * CHUNK, CHUNK)
        for d in range(1, groups):
            k = lax.rem(me + d, groups)
            pltpu.make_async_remote_copy(
                src_ref=slots.at[part, :, :, cols_of(k)],
                dst_ref=out_hbm.at[pl.ds(me * group_size + c * CHUNK, CHUNK)],
                send_sem=send_sems.at[d - 1],
                recv_sem=recv_sems.at[d - 1],
                device_id=(k, row),
                device_id_type=MESH,
            ).start()
        pltpu.make_async_copy(
            slots.at[part, :, :, cols_of(me)],
            out_hbm.at[pl.ds(me * group_size + c * CHUNK, CHUNK)],
            local_sem,
        ).start()

    @pl.when(row > 0)
    def _():
        mask_halo(wall_ref, wall_halo, 0, 0).wait_send()
        mask_halo(infl_ref, infl_halo, 1, 0).wait_send()
        halo_copy(field_hbm.at[:, :, first, :], halo.at[:, :, first, :], 0,
                  halo_recv.at[0, 0], halo_send.at[0]).wait_send()

    @pl.when(row < lines - 1)
    def _():
        mask_halo(wall_ref, wall_halo, 0, 1).wait_send()
        mask_halo(infl_ref, infl_halo, 1, 1).wait_send()
        halo_copy(field_hbm.at[:, :, pl.ds(rows - SUB, SUB), :], halo.at[:, :, last, :], 1,
                  halo_recv.at[1, 0], halo_send.at[1]).wait_send()

    pltpu.make_async_copy(
        slots.at[:, :, :, cols_of(me)], out_hbm.at[pl.ds(me * group_size, group_size)], local_sem
    ).wait()
    for d in range(1, groups):
        k = lax.rem(me + d, groups)
        source = lax.rem(me + groups - d, groups)
        pltpu.make_async_remote_copy(
            src_ref=slots.at[:, :, :, cols_of(k)],
            dst_ref=out_hbm.at[pl.ds(me * group_size, group_size)],
            send_sem=send_sems.at[d - 1],
            recv_sem=recv_sems.at[d - 1],
            device_id=(k, row),
            device_id_type=MESH,
        ).wait_send()
        pltpu.make_async_remote_copy(
            src_ref=slots.at[:, :, :, cols_of(k)],
            dst_ref=out_hbm.at[pl.ds(source * group_size, group_size)],
            send_sem=send_sems.at[d - 1],
            recv_sem=recv_sems.at[d - 1],
            device_id=(k, row),
            device_id_type=MESH,
        ).wait_recv()


def transport_exchange(speed_x, speed_y, inflow_value, field, wall_rows, inflow_rows):
    groups = lax.axis_size("sec")
    lines = lax.axis_size("space")
    group_size, moments, rows, columns = field.shape
    block = columns // groups
    chunks = group_size // CHUNK
    smem = pl.BlockSpec(memory_space=pltpu.SMEM)
    vmem = pl.BlockSpec(memory_space=pltpu.VMEM)
    anywhere = pl.BlockSpec(memory_space=pl.ANY)
    flops = 60 * SUB * field.size
    return pl.pallas_call(
        functools.partial(transport_kernel, groups, lines),
        out_shape=jax.ShapeDtypeStruct((groups * group_size, moments, rows, block), jnp.float32),
        in_specs=[smem, smem, smem, anywhere, vmem, vmem],
        out_specs=anywhere,
        scratch_shapes=[
            pltpu.VMEM((group_size, moments, rows, columns), jnp.float32),
            pltpu.VMEM((group_size, moments, rows, columns), jnp.float32),
            pltpu.VMEM((rows, columns), jnp.int32),
            pltpu.VMEM((rows, columns), jnp.int32),
            pltpu.VMEM((group_size, moments, rows, columns), jnp.float32),
            pltpu.SemaphoreType.DMA((chunks,)),
            pltpu.SemaphoreType.DMA((2, chunks)),
            pltpu.SemaphoreType.DMA((2,)),
            pltpu.SemaphoreType.DMA((2, 2)),
            pltpu.SemaphoreType.DMA((2, 2)),
            pltpu.SemaphoreType.DMA((groups - 1,)),
            pltpu.SemaphoreType.DMA((groups - 1,)),
            pltpu.SemaphoreType.DMA(()),
        ],
        compiler_params=pltpu.CompilerParams(
            collective_id=0, has_side_effects=True, vmem_limit_bytes=60 * 1024 * 1024
        ),
        cost_estimate=pl.CostEstimate(
            flops=flops, bytes_accessed=4 * (field.size * 2), transcendentals=0
        ),
    )(speed_x, speed_y, inflow_value.T, field, wall_rows, inflow_rows)


def post_kernel(rate_ref, tf_ref, coef_ref, share_ref, x_ref, spray_ref, gas_ref):
    span, strip = gas_ref.shape
    rows = tf_ref.shape[0]
    moments = span // rows
    sections = coef_ref.shape[0]
    highest = lax.Precision.HIGH
    lane_rows = lax.broadcasted_iota(jnp.int32, (sections, strip), 0)
    rate = jnp.zeros((sections, strip), jnp.float32)
    for s in range(sections):
        rate = jnp.where(lane_rows == s, rate_ref[s], rate)
    remaining = []
    for r in range(rows):
        factor = rate * tf_ref[pl.ds(r, 1), :]
        for m in range(moments):
            x = x_ref[pl.ds(m * rows + r, sections, stride=span), :]
            evaporated = factor * x
            gas_ref[pl.ds(m * rows + r, 1), :] = jnp.sum(evaporated, axis=0, keepdims=True)
            remaining.append(x - evaporated)
    mass = jnp.concatenate([remaining[r * moments] for r in range(rows)], axis=1)
    merge_rate = jnp.dot(coef_ref[...], mass, precision=highest, preferred_element_type=jnp.float32)
    flux = jnp.concatenate(
        [
            remaining[r * moments + m] * merge_rate[:, r * strip : (r + 1) * strip]
            for r in range(rows)
            for m in range(moments)
        ],
        axis=1,
    )
    gained = jnp.dot(share_ref[...], flux, precision=highest, preferred_element_type=jnp.float32)
    for r in range(rows):
        for m in range(moments):
            at = (r * moments + m) * strip
            spray_ref[pl.ds(m * rows + r, sections, stride=span), :] = (
                remaining[r * moments + m] - flux[:, at : at + strip] + gained[:, at : at + strip]
            )


def evaporate_couple(cell_block, rates, thermal_factor, coefficient, share):
    sections, moments, rows, block = cell_block.shape
    strip = 128
    span = moments * rows
    flat = cell_block.reshape(sections * span, block)
    full = lambda shape: pl.BlockSpec(shape, lambda i: (0, 0))
    spray, gas = pl.pallas_call(
        post_kernel,
        grid=(block // strip,),
        in_specs=[
            pl.BlockSpec(memory_space=pltpu.SMEM),
            pl.BlockSpec((rows, strip), lambda i: (0, i)),
            full((sections, sections)),
            full((sections, sections)),
            pl.BlockSpec((sections * span, strip), lambda i: (0, i)),
        ],
        out_specs=[
            pl.BlockSpec((sections * span, strip), lambda i: (0, i)),
            pl.BlockSpec((span, strip), lambda i: (0, i)),
        ],
        out_shape=[
            jax.ShapeDtypeStruct((sections * span, block), jnp.float32),
            jax.ShapeDtypeStruct((span, block), jnp.float32),
        ],
        cost_estimate=pl.CostEstimate(
            flops=2 * sections * sections * flat.size // sections * (moments + 1) // moments * 6,
            bytes_accessed=8 * flat.size, transcendentals=0,
        ),
    )(rates, thermal_factor, coefficient, share, flat)
    return spray.reshape(sections, moments, rows, block), gas.reshape(moments, rows, block)


def shards(
    droplet_integrals,
    flow_number_lengthwise,
    flow_number_crosswise,
    inflow_boundary_integrals,
    boundary_wall_indicator,
    inflow_indicator,
    collision_coefficient,
    collision_target_share,
    evaporation_speed_stepwise,
    thermal_factor,
):
    cell_block = transport_exchange(
        flow_number_lengthwise, flow_number_crosswise, inflow_boundary_integrals,
        droplet_integrals, boundary_wall_indicator, inflow_indicator,
    )
    spray, gas_source = evaporate_couple(
        cell_block, evaporation_speed_stepwise, thermal_factor,
        collision_coefficient, collision_target_share,
    )
    return (spray, gas_source)


def solution(mesh):
    return jax.shard_map(
        shards,
        mesh=mesh,
        in_specs=(
            P("sec", None, "space", None),
            P("sec"),
            P("sec"),
            P("sec", None),
            P("space", None),
            P("space", None),
            P(),
            P(),
            P(),
            P("space", "sec"),
        ),
        out_specs=(P(None, None, "space", "sec"), P(None, "space", "sec")),
        check_vma=False,
    )
```

```python
import functools

import jax
import jax.numpy as jnp
from jax import lax
from jax.experimental import pallas as pl
from jax.experimental.pallas import tpu as pltpu
from jax.sharding import PartitionSpec as P

SUB = 4
CHUNK = 4
RELAYED = (2, 3)
PLANE = 4
MESH = pl.DeviceIdType.MESH


def transport_kernel(
    groups, lines,
    ux_ref, uy_ref, iv_ref, field_hbm, wall_ref, infl_ref,
    out_hbm,
    local, halo, wall_halo, infl_halo, slots, relay,
    load_sems, halo_recv, halo_send, mask_recv, mask_send, send_sems, recv_sems, local_sem,
    relay_recv, relay_send,
):
    group_size, moments, rows, columns = field_hbm.shape
    span = 2 * rows
    block = columns // groups
    chunks = group_size // CHUNK
    me = lax.axis_index("sec")
    row = lax.axis_index("space")
    has_west = (row + lines - 1) // lines
    has_east = 1 - row // (lines - 1)
    west = (me, row - 1)
    east = (me, row + 1)
    first = pl.ds(0, SUB)
    last = pl.ds(SUB, SUB)
    at = lambda offset: (me, row + offset)

    res = row % PLANE
    left_edge = (res == PLANE - 1) & (row < lines - 1)
    right_edge = (res == 0) & (row > 0)
    east_first = (res == PLANE - 2) & (row + 2 < lines)
    east_second = (res == PLANE - 2) & (row >= PLANE + 2)
    west_first = (res == 1) & (row >= PLANE + 1)
    west_second = (res == 1) & (row + PLANE - 1 < lines)
    greetings = [
        (row > 0, -1), (row < lines - 1, 1),
        (left_edge, -2), (right_edge, 2),
        (east_first, PLANE), (east_second, -PLANE), (east_second, -2),
        (west_first, -PLANE), (west_second, PLANE), (west_second, 2),
    ]

    loads = []
    for c in range(chunks):
        part = pl.ds(c * CHUNK, CHUNK)
        load = pltpu.make_async_copy(field_hbm.at[part], local.at[part], load_sems.at[c])
        load.start()
        loads.append(load)

    @pl.when(row == 0)
    def _():
        halo[:, :, last, :] = jnp.zeros((group_size, moments, SUB, columns), jnp.float32)
        wall_halo[last, :] = jnp.ones((SUB, columns), jnp.int32)
        infl_halo[last, :] = jnp.zeros((SUB, columns), jnp.int32)

    @pl.when(row == lines - 1)
    def _():
        halo[:, :, first, :] = jnp.zeros((group_size, moments, SUB, columns), jnp.float32)
        wall_halo[first, :] = jnp.ones((SUB, columns), jnp.int32)
        infl_halo[first, :] = jnp.zeros((SUB, columns), jnp.int32)

    barrier = pltpu.get_barrier_semaphore()
    for d in range(1, groups):
        pl.semaphore_signal(barrier, 1, device_id=(lax.rem(me + d, groups), row), device_id_type=MESH)
    for cond, offset in greetings:
        @pl.when(cond)
        def _():
            pl.semaphore_signal(barrier, 1, device_id=at(offset), device_id_type=MESH)
    same = lambda v: 1 - ((res - v + PLANE) % PLANE + PLANE - 1) // PLANE
    past = lambda a: (row - a + lines) // lines
    peers = (
        groups - 1 + has_west + has_east
        + same(PLANE - 1) * has_east + same(0) * has_west
        + same(PLANE - 2) * (1 - past(lines - 2)) + 2 * same(PLANE - 2) * past(PLANE + 2)
        + same(1) * past(PLANE + 1) + 2 * same(1) * (1 - past(lines - PLANE + 1))
    )
    pl.semaphore_wait(barrier, peers)

    def halo_copy(src, dst, target, sem_recv, sem_send):
        return pltpu.make_async_remote_copy(
            src_ref=src, dst_ref=dst, send_sem=sem_send, recv_sem=sem_recv,
            device_id=target, device_id_type=MESH,
        )

    def field_halo(c, direction):
        part = pl.ds(c * CHUNK, CHUNK)
        if direction == 0:
            return halo_copy(field_hbm.at[part, :, first, :], halo.at[part, :, first, :], west,
                             halo_recv.at[0, c], halo_send.at[0])
        return halo_copy(field_hbm.at[part, :, pl.ds(rows - SUB, SUB), :], halo.at[part, :, last, :], east,
                         halo_recv.at[1, c], halo_send.at[1])

    def relay_part(c):
        return pl.ds(RELAYED.index(c) * CHUNK, CHUNK)

    def relay_in(c, direction):
        part = pl.ds(c * CHUNK, CHUNK)
        if direction == 0:
            return halo_copy(field_hbm.at[part, :, first, :], relay.at[0, relay_part(c)], east,
                             relay_recv.at[0, RELAYED.index(c)], halo_send.at[0])
        return halo_copy(field_hbm.at[part, :, pl.ds(rows - SUB, SUB), :], relay.at[0, relay_part(c)], west,
                         relay_recv.at[0, RELAYED.index(c)], halo_send.at[1])

    def relay_on(c, stage, offset, direction):
        j = RELAYED.index(c)
        part = pl.ds(c * CHUNK, CHUNK)
        if stage == 0:
            return halo_copy(relay.at[0, relay_part(c)], relay.at[1, relay_part(c)], at(offset),
                             relay_recv.at[1, j], relay_send.at[0])
        return halo_copy(relay.at[1, relay_part(c)], halo.at[part, :, first if direction == 0 else last, :],
                         at(offset), halo_recv.at[direction, c], relay_send.at[1])

    def mask_halo(ref, store, k, direction):
        if direction == 0:
            return halo_copy(ref.at[first, :], store.at[first, :], west, mask_recv.at[k, 0], mask_send.at[k, 0])
        return halo_copy(ref.at[pl.ds(rows - SUB, SUB), :], store.at[last, :], east,
                         mask_recv.at[k, 1], mask_send.at[k, 1])

    @pl.when(row > 0)
    def _():
        mask_halo(wall_ref, wall_halo, 0, 0).start()
        mask_halo(infl_ref, infl_halo, 1, 0).start()
        for c in range(chunks):
            if c in RELAYED:
                @pl.when(jnp.logical_not(right_edge))
                def _():
                    field_halo(c, 0).start()

                @pl.when(right_edge)
                def _():
                    relay_in(c, 0).start()
            else:
                field_halo(c, 0).start()

    @pl.when(row < lines - 1)
    def _():
        mask_halo(wall_ref, wall_halo, 0, 1).start()
        mask_halo(infl_ref, infl_halo, 1, 1).start()
        for c in range(chunks):
            if c in RELAYED:
                @pl.when(jnp.logical_not(left_edge))
                def _():
                    field_halo(c, 1).start()

                @pl.when(left_edge)
                def _():
                    relay_in(c, 1).start()
            else:
                field_halo(c, 1).start()

    @pl.when(row < lines - 1)
    def _():
        mask_halo(wall_ref, wall_halo, 0, 0).wait_recv()
        mask_halo(infl_ref, infl_halo, 1, 0).wait_recv()

    @pl.when(row > 0)
    def _():
        mask_halo(wall_ref, wall_halo, 0, 1).wait_recv()
        mask_halo(infl_ref, infl_halo, 1, 1).wait_recv()

    def forward(stage):
        for c in RELAYED:
            if stage == 0:
                @pl.when(east_first)
                def _():
                    relay_in(c, 1).wait_recv()
                    relay_on(c, 0, PLANE, 1).start()

                @pl.when(west_first)
                def _():
                    relay_in(c, 0).wait_recv()
                    relay_on(c, 0, -PLANE, 0).start()
            else:
                @pl.when(east_second)
                def _():
                    relay_on(c, 0, PLANE, 1).wait_recv()
                    relay_on(c, 1, -2, 1).start()

                @pl.when(west_second)
                def _():
                    relay_on(c, 0, -PLANE, 0).wait_recv()
                    relay_on(c, 1, 2, 0).start()

    def cols_of(k):
        return pl.ds(pl.multiple_of(k * block, block), block)

    for c in range(chunks):
        if c == 1:
            forward(0)
        if c == 2:
            forward(1)
        loads[c].wait()

        @pl.when(row < lines - 1)
        def _():
            field_halo(c, 0).wait_recv()

        @pl.when(row > 0)
        def _():
            field_halo(c, 1).wait_recv()

        def body(i, carry):
            s = c * CHUNK + i
            ux = ux_ref[s]
            uy = uy_ref[s]
            px = jnp.maximum(ux, 0.0)
            nx = jnp.minimum(ux, 0.0)
            py = jnp.maximum(uy, 0.0)
            ny = jnp.minimum(uy, 0.0)
            for m in range(moments):
                q = jnp.concatenate([local[s, m], halo[s, m]], axis=0)
                iv = iv_ref[m, s]
                for step in range(SUB):
                    col = lax.broadcasted_iota(jnp.int32, q.shape, 1)
                    western = pltpu.roll(q, 1, 0)
                    eastern = pltpu.roll(q, span - 1, 0)
                    southern = jnp.where(col == 0, 0.0, pltpu.roll(q, 1, 1))
                    northern = jnp.where(col == columns - 1, 0.0, pltpu.roll(q, columns - 1, 1))
                    t = q - px * (q - western) - nx * (eastern - q)
                    t = t - py * (q - southern) - ny * (northern - q)
                    inflow_rows = jnp.concatenate([infl_ref[...], infl_halo[...]], axis=0)
                    wall_rows = jnp.concatenate([wall_ref[...], wall_halo[...]], axis=0)
                    t = jnp.where(inflow_rows > 0, iv, t)
                    q = jnp.where(wall_rows > 0, 0.0, t)
                slots[s, m] = q[:rows]
            return carry

        lax.fori_loop(0, CHUNK, body, 0)

        part = pl.ds(c * CHUNK, CHUNK)
        for d in range(1, groups):
            k = lax.rem(me + d, groups)
            pltpu.make_async_remote_copy(
                src_ref=slots.at[part, :, :, cols_of(k)],
                dst_ref=out_hbm.at[pl.ds(me * group_size + c * CHUNK, CHUNK)],
                send_sem=send_sems.at[d - 1],
                recv_sem=recv_sems.at[d - 1],
                device_id=(k, row),
                device_id_type=MESH,
            ).start()
        pltpu.make_async_copy(
            slots.at[part, :, :, cols_of(me)],
            out_hbm.at[pl.ds(me * group_size + c * CHUNK, CHUNK)],
            local_sem,
        ).start()

    @pl.when(row > 0)
    def _():
        mask_halo(wall_ref, wall_halo, 0, 0).wait_send()
        mask_halo(infl_ref, infl_halo, 1, 0).wait_send()
        halo_copy(field_hbm.at[:, :, first, :], halo.at[:, :, first, :], west,
                  halo_recv.at[0, 0], halo_send.at[0]).wait_send()

    @pl.when(row < lines - 1)
    def _():
        mask_halo(wall_ref, wall_halo, 0, 1).wait_send()
        mask_halo(infl_ref, infl_halo, 1, 1).wait_send()
        halo_copy(field_hbm.at[:, :, pl.ds(rows - SUB, SUB), :], halo.at[:, :, last, :], east,
                  halo_recv.at[1, 0], halo_send.at[1]).wait_send()

    for stage, conds in ((0, (east_first, west_first)), (1, (east_second, west_second))):
        for cond in conds:
            @pl.when(cond)
            def _():
                halo_copy(relay.at[stage], relay.at[stage], west,
                          relay_recv.at[0, 0], relay_send.at[stage]).wait_send()

    pltpu.make_async_copy(
        slots.at[:, :, :, cols_of(me)], out_hbm.at[pl.ds(me * group_size, group_size)], local_sem
    ).wait()
    for d in range(1, groups):
        k = lax.rem(me + d, groups)
        source = lax.rem(me + groups - d, groups)
        pltpu.make_async_remote_copy(
            src_ref=slots.at[:, :, :, cols_of(k)],
            dst_ref=out_hbm.at[pl.ds(me * group_size, group_size)],
            send_sem=send_sems.at[d - 1],
            recv_sem=recv_sems.at[d - 1],
            device_id=(k, row),
            device_id_type=MESH,
        ).wait_send()
        pltpu.make_async_remote_copy(
            src_ref=slots.at[:, :, :, cols_of(k)],
            dst_ref=out_hbm.at[pl.ds(source * group_size, group_size)],
            send_sem=send_sems.at[d - 1],
            recv_sem=recv_sems.at[d - 1],
            device_id=(k, row),
            device_id_type=MESH,
        ).wait_recv()


def transport_exchange(speed_x, speed_y, inflow_value, field, wall_rows, inflow_rows):
    groups = lax.axis_size("sec")
    lines = lax.axis_size("space")
    group_size, moments, rows, columns = field.shape
    block = columns // groups
    chunks = group_size // CHUNK
    smem = pl.BlockSpec(memory_space=pltpu.SMEM)
    vmem = pl.BlockSpec(memory_space=pltpu.VMEM)
    anywhere = pl.BlockSpec(memory_space=pl.ANY)
    flops = 60 * SUB * field.size
    return pl.pallas_call(
        functools.partial(transport_kernel, groups, lines),
        out_shape=jax.ShapeDtypeStruct((groups * group_size, moments, rows, block), jnp.float32),
        in_specs=[smem, smem, smem, anywhere, vmem, vmem],
        out_specs=anywhere,
        scratch_shapes=[
            pltpu.VMEM((group_size, moments, rows, columns), jnp.float32),
            pltpu.VMEM((group_size, moments, rows, columns), jnp.float32),
            pltpu.VMEM((rows, columns), jnp.int32),
            pltpu.VMEM((rows, columns), jnp.int32),
            pltpu.VMEM((group_size, moments, rows, columns), jnp.float32),
            pltpu.VMEM((2, len(RELAYED) * CHUNK, moments, SUB, columns), jnp.float32),
            pltpu.SemaphoreType.DMA((chunks,)),
            pltpu.SemaphoreType.DMA((2, chunks)),
            pltpu.SemaphoreType.DMA((2,)),
            pltpu.SemaphoreType.DMA((2, 2)),
            pltpu.SemaphoreType.DMA((2, 2)),
            pltpu.SemaphoreType.DMA((groups - 1,)),
            pltpu.SemaphoreType.DMA((groups - 1,)),
            pltpu.SemaphoreType.DMA(()),
            pltpu.SemaphoreType.DMA((2, len(RELAYED))),
            pltpu.SemaphoreType.DMA((2,)),
        ],
        compiler_params=pltpu.CompilerParams(
            collective_id=0, has_side_effects=True, vmem_limit_bytes=60 * 1024 * 1024
        ),
        cost_estimate=pl.CostEstimate(
            flops=flops, bytes_accessed=4 * (field.size * 2), transcendentals=0
        ),
    )(speed_x, speed_y, inflow_value.T, field, wall_rows, inflow_rows)


def post_kernel(rate_ref, tf_ref, coef_ref, share_ref, x_ref, spray_ref, gas_ref):
    span, strip = gas_ref.shape
    rows = tf_ref.shape[0]
    moments = span // rows
    sections = coef_ref.shape[0]
    highest = lax.Precision.HIGH
    lane_rows = lax.broadcasted_iota(jnp.int32, (sections, strip), 0)
    rate = jnp.zeros((sections, strip), jnp.float32)
    for s in range(sections):
        rate = jnp.where(lane_rows == s, rate_ref[s], rate)
    remaining = []
    for r in range(rows):
        factor = rate * tf_ref[pl.ds(r, 1), :]
        for m in range(moments):
            x = x_ref[pl.ds(m * rows + r, sections, stride=span), :]
            evaporated = factor * x
            gas_ref[pl.ds(m * rows + r, 1), :] = jnp.sum(evaporated, axis=0, keepdims=True)
            remaining.append(x - evaporated)
    mass = jnp.concatenate([remaining[r * moments] for r in range(rows)], axis=1)
    merge_rate = jnp.dot(coef_ref[...], mass, precision=highest, preferred_element_type=jnp.float32)
    flux = jnp.concatenate(
        [
            remaining[r * moments + m] * merge_rate[:, r * strip : (r + 1) * strip]
            for r in range(rows)
            for m in range(moments)
        ],
        axis=1,
    )
    gained = jnp.dot(share_ref[...], flux, precision=highest, preferred_element_type=jnp.float32)
    for r in range(rows):
        for m in range(moments):
            at = (r * moments + m) * strip
            spray_ref[pl.ds(m * rows + r, sections, stride=span), :] = (
                remaining[r * moments + m] - flux[:, at : at + strip] + gained[:, at : at + strip]
            )


def evaporate_couple(cell_block, rates, thermal_factor, coefficient, share):
    sections, moments, rows, block = cell_block.shape
    strip = 128
    span = moments * rows
    flat = cell_block.reshape(sections * span, block)
    full = lambda shape: pl.BlockSpec(shape, lambda i: (0, 0))
    spray, gas = pl.pallas_call(
        post_kernel,
        grid=(block // strip,),
        in_specs=[
            pl.BlockSpec(memory_space=pltpu.SMEM),
            pl.BlockSpec((rows, strip), lambda i: (0, i)),
            full((sections, sections)),
            full((sections, sections)),
            pl.BlockSpec((sections * span, strip), lambda i: (0, i)),
        ],
        out_specs=[
            pl.BlockSpec((sections * span, strip), lambda i: (0, i)),
            pl.BlockSpec((span, strip), lambda i: (0, i)),
        ],
        out_shape=[
            jax.ShapeDtypeStruct((sections * span, block), jnp.float32),
            jax.ShapeDtypeStruct((span, block), jnp.float32),
        ],
        cost_estimate=pl.CostEstimate(
            flops=2 * sections * sections * flat.size // sections * (moments + 1) // moments * 6,
            bytes_accessed=8 * flat.size, transcendentals=0,
        ),
    )(rates, thermal_factor, coefficient, share, flat)
    return spray.reshape(sections, moments, rows, block), gas.reshape(moments, rows, block)


def shards(
    droplet_integrals,
    flow_number_lengthwise,
    flow_number_crosswise,
    inflow_boundary_integrals,
    boundary_wall_indicator,
    inflow_indicator,
    collision_coefficient,
    collision_target_share,
    evaporation_speed_stepwise,
    thermal_factor,
):
    cell_block = transport_exchange(
        flow_number_lengthwise, flow_number_crosswise, inflow_boundary_integrals,
        droplet_integrals, boundary_wall_indicator, inflow_indicator,
    )
    spray, gas_source = evaporate_couple(
        cell_block, evaporation_speed_stepwise, thermal_factor,
        collision_coefficient, collision_target_share,
    )
    return (spray, gas_source)


def solution(mesh):
    return jax.shard_map(
        shards,
        mesh=mesh,
        in_specs=(
            P("sec", None, "space", None),
            P("sec"),
            P("sec"),
            P("sec", None),
            P("space", None),
            P("space", None),
            P(),
            P(),
            P(),
            P("space", "sec"),
        ),
        out_specs=(P(None, None, "space", "sec"), P(None, "space", "sec")),
        check_vma=False,
    )
```

```python
import functools

import jax
import jax.numpy as jnp
from jax import lax
from jax.experimental import pallas as pl
from jax.experimental.pallas import tpu as pltpu
from jax.sharding import PartitionSpec as P

SUB = 4
CHUNK = 4
RELAYED = (2, 3)
PLANE = 4
MESH = pl.DeviceIdType.MESH


def transport_kernel(
    groups, lines,
    ux_ref, uy_ref, iv_ref, field_hbm, wall_ref, infl_ref,
    out_hbm,
    local, halo, wall_halo, infl_halo, slots, relay,
    load_sems, halo_recv, halo_send, mask_recv, mask_send, send_sems, recv_sems, local_sem,
    relay_recv, relay_send,
):
    group_size, moments, rows, columns = field_hbm.shape
    span = 2 * rows
    block = columns // groups
    chunks = group_size // CHUNK
    me = lax.axis_index("sec")
    row = lax.axis_index("space")
    has_west = (row + lines - 1) // lines
    has_east = 1 - row // (lines - 1)
    west = (me, row - 1)
    east = (me, row + 1)
    first = pl.ds(0, SUB)
    last = pl.ds(SUB, SUB)
    res = row % PLANE
    edge_low = (res == PLANE - 1) & (row < lines - 1)
    edge_high = (res == 0) & (row > 0)
    relay_low = (res == PLANE - 2) & (row + 2 < lines)
    relay_high = (res == 1) & (row >= PLANE + 1)

    loads = []
    for c in range(chunks):
        part = pl.ds(c * CHUNK, CHUNK)
        load = pltpu.make_async_copy(field_hbm.at[part], local.at[part], load_sems.at[c])
        load.start()
        loads.append(load)

    @pl.when(row == 0)
    def _():
        halo[:, :, last, :] = jnp.zeros((group_size, moments, SUB, columns), jnp.float32)
        wall_halo[last, :] = jnp.ones((SUB, columns), jnp.int32)
        infl_halo[last, :] = jnp.zeros((SUB, columns), jnp.int32)

    @pl.when(row == lines - 1)
    def _():
        halo[:, :, first, :] = jnp.zeros((group_size, moments, SUB, columns), jnp.float32)
        wall_halo[first, :] = jnp.ones((SUB, columns), jnp.int32)
        infl_halo[first, :] = jnp.zeros((SUB, columns), jnp.int32)

    barrier = pltpu.get_barrier_semaphore()
    for d in range(1, groups):
        pl.semaphore_signal(barrier, 1, device_id=(lax.rem(me + d, groups), row), device_id_type=MESH)

    @pl.when(row > 0)
    def _():
        pl.semaphore_signal(barrier, 1, device_id=west, device_id_type=MESH)

    @pl.when(row < lines - 1)
    def _():
        pl.semaphore_signal(barrier, 1, device_id=east, device_id_type=MESH)

    pl.semaphore_wait(barrier, groups - 1 + has_west + has_east)

    def halo_copy(src, dst, direction, sem_recv, sem_send):
        return pltpu.make_async_remote_copy(
            src_ref=src, dst_ref=dst, send_sem=sem_send, recv_sem=sem_recv,
            device_id=west if direction == 0 else east, device_id_type=MESH,
        )

    def field_halo(c, direction):
        part = pl.ds(c * CHUNK, CHUNK)
        if direction == 0:
            return halo_copy(field_hbm.at[part, :, first, :], halo.at[part, :, first, :], 0,
                             halo_recv.at[0, c], halo_send.at[0])
        return halo_copy(field_hbm.at[part, :, pl.ds(rows - SUB, SUB), :], halo.at[part, :, last, :], 1,
                         halo_recv.at[1, c], halo_send.at[1])

    def mask_halo(ref, store, k, direction):
        if direction == 0:
            return halo_copy(ref.at[first, :], store.at[first, :], 0, mask_recv.at[k, 0], mask_send.at[k, 0])
        return halo_copy(ref.at[pl.ds(rows - SUB, SUB), :], store.at[last, :], 1,
                         mask_recv.at[k, 1], mask_send.at[k, 1])

    @pl.when(row > 0)
    def _():
        mask_halo(wall_ref, wall_halo, 0, 0).start()
        mask_halo(infl_ref, infl_halo, 1, 0).start()
        for c in range(chunks):
            field_halo(c, 0).start()

    @pl.when(row < lines - 1)
    def _():
        mask_halo(wall_ref, wall_halo, 0, 1).start()
        mask_halo(infl_ref, infl_halo, 1, 1).start()
        for c in range(chunks):
            field_halo(c, 1).start()

    @pl.when(row < lines - 1)
    def _():
        mask_halo(wall_ref, wall_halo, 0, 0).wait_recv()
        mask_halo(infl_ref, infl_halo, 1, 0).wait_recv()

    @pl.when(row > 0)
    def _():
        mask_halo(wall_ref, wall_halo, 0, 1).wait_recv()
        mask_halo(infl_ref, infl_halo, 1, 1).wait_recv()

    def cols_of(k):
        return pl.ds(pl.multiple_of(k * block, block), block)

    for c in range(chunks):
        loads[c].wait()

        @pl.when(row < lines - 1)
        def _():
            field_halo(c, 0).wait_recv()

        @pl.when(row > 0)
        def _():
            field_halo(c, 1).wait_recv()

        def body(i, carry):
            s = c * CHUNK + i
            ux = ux_ref[s]
            uy = uy_ref[s]
            px = jnp.maximum(ux, 0.0)
            nx = jnp.minimum(ux, 0.0)
            py = jnp.maximum(uy, 0.0)
            ny = jnp.minimum(uy, 0.0)
            for m in range(moments):
                q = jnp.concatenate([local[s, m], halo[s, m]], axis=0)
                iv = iv_ref[m, s]
                for step in range(SUB):
                    col = lax.broadcasted_iota(jnp.int32, q.shape, 1)
                    western = pltpu.roll(q, 1, 0)
                    eastern = pltpu.roll(q, span - 1, 0)
                    southern = jnp.where(col == 0, 0.0, pltpu.roll(q, 1, 1))
                    northern = jnp.where(col == columns - 1, 0.0, pltpu.roll(q, columns - 1, 1))
                    t = q - px * (q - western) - nx * (eastern - q)
                    t = t - py * (q - southern) - ny * (northern - q)
                    inflow_rows = jnp.concatenate([infl_ref[...], infl_halo[...]], axis=0)
                    wall_rows = jnp.concatenate([wall_ref[...], wall_halo[...]], axis=0)
                    t = jnp.where(inflow_rows > 0, iv, t)
                    q = jnp.where(wall_rows > 0, 0.0, t)
                slots[s, m] = q[:rows]
            return carry

        lax.fori_loop(0, CHUNK, body, 0)

        part = pl.ds(c * CHUNK, CHUNK)

        def direct():
            for d in range(1, groups):
                k = lax.rem(me + d, groups)
                pltpu.make_async_remote_copy(
                    src_ref=slots.at[part, :, :, cols_of(k)],
                    dst_ref=out_hbm.at[pl.ds(me * group_size + c * CHUNK, CHUNK)],
                    send_sem=send_sems.at[d - 1],
                    recv_sem=recv_sems.at[d - 1],
                    device_id=(k, row),
                    device_id_type=MESH,
                ).start()

        if c in RELAYED:
            j = RELAYED.index(c)

            def via(offset):
                for d in range(1, groups):
                    k = lax.rem(me + d, groups)
                    pltpu.make_async_remote_copy(
                        src_ref=slots.at[part, :, :, cols_of(k)],
                        dst_ref=relay.at[0, j, d - 1],
                        send_sem=send_sems.at[d - 1],
                        recv_sem=relay_recv.at[0, j, d - 1],
                        device_id=(me, row + offset),
                        device_id_type=MESH,
                    ).start()

            pl.when(edge_low)(lambda: via(-1))
            pl.when(edge_high)(lambda: via(1))
            pl.when(jnp.logical_not(edge_low | edge_high))(direct)
        else:
            direct()
        pltpu.make_async_copy(
            slots.at[part, :, :, cols_of(me)],
            out_hbm.at[pl.ds(me * group_size + c * CHUNK, CHUNK)],
            local_sem,
        ).start()

    def forward(offset):
        for j in range(len(RELAYED)):
            for d in range(1, groups):
                pltpu.make_async_remote_copy(
                    src_ref=slots.at[pl.ds(0, CHUNK), :, :, cols_of(me)],
                    dst_ref=relay.at[0, j, d - 1],
                    send_sem=relay_send.at[0],
                    recv_sem=relay_recv.at[0, j, d - 1],
                    device_id=(me, row + offset),
                    device_id_type=MESH,
                ).wait_recv()
                pltpu.make_async_remote_copy(
                    src_ref=relay.at[0, j, d - 1],
                    dst_ref=relay.at[1, j, d - 1],
                    send_sem=relay_send.at[0],
                    recv_sem=relay_recv.at[1, j, d - 1],
                    device_id=(lax.rem(me + d, groups), row),
                    device_id_type=MESH,
                ).start()
        for j, c in enumerate(RELAYED):
            for d in range(1, groups):
                source = lax.rem(me + groups - d, groups)
                pltpu.make_async_remote_copy(
                    src_ref=relay.at[0, j, d - 1],
                    dst_ref=relay.at[1, j, d - 1],
                    send_sem=relay_send.at[0],
                    recv_sem=relay_recv.at[1, j, d - 1],
                    device_id=(me, row),
                    device_id_type=MESH,
                ).wait_recv()
                pltpu.make_async_remote_copy(
                    src_ref=relay.at[1, j, d - 1],
                    dst_ref=out_hbm.at[pl.ds(source * group_size + c * CHUNK, CHUNK)],
                    send_sem=relay_send.at[1],
                    recv_sem=recv_sems.at[d - 1],
                    device_id=(me, row + offset),
                    device_id_type=MESH,
                ).start()
        for stage in range(2):
            pltpu.make_async_remote_copy(
                src_ref=relay.at[stage], dst_ref=relay.at[stage],
                send_sem=relay_send.at[stage], recv_sem=relay_recv.at[stage, 0, 0],
                device_id=(me, row + offset), device_id_type=MESH,
            ).wait_send()

    pl.when(relay_low)(lambda: forward(1))
    pl.when(relay_high)(lambda: forward(-1))

    @pl.when(row > 0)
    def _():
        mask_halo(wall_ref, wall_halo, 0, 0).wait_send()
        mask_halo(infl_ref, infl_halo, 1, 0).wait_send()
        halo_copy(field_hbm.at[:, :, first, :], halo.at[:, :, first, :], 0,
                  halo_recv.at[0, 0], halo_send.at[0]).wait_send()

    @pl.when(row < lines - 1)
    def _():
        mask_halo(wall_ref, wall_halo, 0, 1).wait_send()
        mask_halo(infl_ref, infl_halo, 1, 1).wait_send()
        halo_copy(field_hbm.at[:, :, pl.ds(rows - SUB, SUB), :], halo.at[:, :, last, :], 1,
                  halo_recv.at[1, 0], halo_send.at[1]).wait_send()

    pltpu.make_async_copy(
        slots.at[:, :, :, cols_of(me)], out_hbm.at[pl.ds(me * group_size, group_size)], local_sem
    ).wait()
    for d in range(1, groups):
        k = lax.rem(me + d, groups)
        source = lax.rem(me + groups - d, groups)
        pltpu.make_async_remote_copy(
            src_ref=slots.at[:, :, :, cols_of(k)],
            dst_ref=out_hbm.at[pl.ds(me * group_size, group_size)],
            send_sem=send_sems.at[d - 1],
            recv_sem=recv_sems.at[d - 1],
            device_id=(k, row),
            device_id_type=MESH,
        ).wait_send()
        pltpu.make_async_remote_copy(
            src_ref=slots.at[:, :, :, cols_of(k)],
            dst_ref=out_hbm.at[pl.ds(source * group_size, group_size)],
            send_sem=send_sems.at[d - 1],
            recv_sem=recv_sems.at[d - 1],
            device_id=(k, row),
            device_id_type=MESH,
        ).wait_recv()


def transport_exchange(speed_x, speed_y, inflow_value, field, wall_rows, inflow_rows):
    groups = lax.axis_size("sec")
    lines = lax.axis_size("space")
    group_size, moments, rows, columns = field.shape
    block = columns // groups
    chunks = group_size // CHUNK
    smem = pl.BlockSpec(memory_space=pltpu.SMEM)
    vmem = pl.BlockSpec(memory_space=pltpu.VMEM)
    anywhere = pl.BlockSpec(memory_space=pl.ANY)
    flops = 60 * SUB * field.size
    return pl.pallas_call(
        functools.partial(transport_kernel, groups, lines),
        out_shape=jax.ShapeDtypeStruct((groups * group_size, moments, rows, block), jnp.float32),
        in_specs=[smem, smem, smem, anywhere, vmem, vmem],
        out_specs=anywhere,
        scratch_shapes=[
            pltpu.VMEM((group_size, moments, rows, columns), jnp.float32),
            pltpu.VMEM((group_size, moments, rows, columns), jnp.float32),
            pltpu.VMEM((rows, columns), jnp.int32),
            pltpu.VMEM((rows, columns), jnp.int32),
            pltpu.VMEM((group_size, moments, rows, columns), jnp.float32),
            pltpu.VMEM((2, len(RELAYED), groups - 1, CHUNK, moments, rows, block), jnp.float32),
            pltpu.SemaphoreType.DMA((chunks,)),
            pltpu.SemaphoreType.DMA((2, chunks)),
            pltpu.SemaphoreType.DMA((2,)),
            pltpu.SemaphoreType.DMA((2, 2)),
            pltpu.SemaphoreType.DMA((2, 2)),
            pltpu.SemaphoreType.DMA((groups - 1,)),
            pltpu.SemaphoreType.DMA((groups - 1,)),
            pltpu.SemaphoreType.DMA(()),
            pltpu.SemaphoreType.DMA((2, len(RELAYED), groups - 1)),
            pltpu.SemaphoreType.DMA((2,)),
        ],
        compiler_params=pltpu.CompilerParams(
            collective_id=0, has_side_effects=True, vmem_limit_bytes=60 * 1024 * 1024
        ),
        cost_estimate=pl.CostEstimate(
            flops=flops, bytes_accessed=4 * (field.size * 2), transcendentals=0
        ),
    )(speed_x, speed_y, inflow_value.T, field, wall_rows, inflow_rows)


def post_kernel(rate_ref, tf_ref, coef_ref, share_ref, x_ref, spray_ref, gas_ref):
    span, strip = gas_ref.shape
    rows = tf_ref.shape[0]
    moments = span // rows
    sections = coef_ref.shape[0]
    highest = lax.Precision.HIGH
    lane_rows = lax.broadcasted_iota(jnp.int32, (sections, strip), 0)
    rate = jnp.zeros((sections, strip), jnp.float32)
    for s in range(sections):
        rate = jnp.where(lane_rows == s, rate_ref[s], rate)
    remaining = []
    for r in range(rows):
        factor = rate * tf_ref[pl.ds(r, 1), :]
        for m in range(moments):
            x = x_ref[pl.ds(m * rows + r, sections, stride=span), :]
            evaporated = factor * x
            gas_ref[pl.ds(m * rows + r, 1), :] = jnp.sum(evaporated, axis=0, keepdims=True)
            remaining.append(x - evaporated)
    mass = jnp.concatenate([remaining[r * moments] for r in range(rows)], axis=1)
    merge_rate = jnp.dot(coef_ref[...], mass, precision=highest, preferred_element_type=jnp.float32)
    flux = jnp.concatenate(
        [
            remaining[r * moments + m] * merge_rate[:, r * strip : (r + 1) * strip]
            for r in range(rows)
            for m in range(moments)
        ],
        axis=1,
    )
    gained = jnp.dot(share_ref[...], flux, precision=highest, preferred_element_type=jnp.float32)
    for r in range(rows):
        for m in range(moments):
            at = (r * moments + m) * strip
            spray_ref[pl.ds(m * rows + r, sections, stride=span), :] = (
                remaining[r * moments + m] - flux[:, at : at + strip] + gained[:, at : at + strip]
            )


def evaporate_couple(cell_block, rates, thermal_factor, coefficient, share):
    sections, moments, rows, block = cell_block.shape
    strip = 128
    span = moments * rows
    flat = cell_block.reshape(sections * span, block)
    full = lambda shape: pl.BlockSpec(shape, lambda i: (0, 0))
    spray, gas = pl.pallas_call(
        post_kernel,
        grid=(block // strip,),
        in_specs=[
            pl.BlockSpec(memory_space=pltpu.SMEM),
            pl.BlockSpec((rows, strip), lambda i: (0, i)),
            full((sections, sections)),
            full((sections, sections)),
            pl.BlockSpec((sections * span, strip), lambda i: (0, i)),
        ],
        out_specs=[
            pl.BlockSpec((sections * span, strip), lambda i: (0, i)),
            pl.BlockSpec((span, strip), lambda i: (0, i)),
        ],
        out_shape=[
            jax.ShapeDtypeStruct((sections * span, block), jnp.float32),
            jax.ShapeDtypeStruct((span, block), jnp.float32),
        ],
        cost_estimate=pl.CostEstimate(
            flops=2 * sections * sections * flat.size // sections * (moments + 1) // moments * 6,
            bytes_accessed=8 * flat.size, transcendentals=0,
        ),
    )(rates, thermal_factor, coefficient, share, flat)
    return spray.reshape(sections, moments, rows, block), gas.reshape(moments, rows, block)


def shards(
    droplet_integrals,
    flow_number_lengthwise,
    flow_number_crosswise,
    inflow_boundary_integrals,
    boundary_wall_indicator,
    inflow_indicator,
    collision_coefficient,
    collision_target_share,
    evaporation_speed_stepwise,
    thermal_factor,
):
    cell_block = transport_exchange(
        flow_number_lengthwise, flow_number_crosswise, inflow_boundary_integrals,
        droplet_integrals, boundary_wall_indicator, inflow_indicator,
    )
    spray, gas_source = evaporate_couple(
        cell_block, evaporation_speed_stepwise, thermal_factor,
        collision_coefficient, collision_target_share,
    )
    return (spray, gas_source)


def solution(mesh):
    return jax.shard_map(
        shards,
        mesh=mesh,
        in_specs=(
            P("sec", None, "space", None),
            P("sec"),
            P("sec"),
            P("sec", None),
            P("space", None),
            P("space", None),
            P(),
            P(),
            P(),
            P("space", "sec"),
        ),
        out_specs=(P(None, None, "space", "sec"), P(None, "space", "sec")),
        check_vma=False,
    )
```

```python
import functools

import jax
import jax.numpy as jnp
from jax import lax
from jax.experimental import pallas as pl
from jax.experimental.pallas import tpu as pltpu
from jax.sharding import PartitionSpec as P

SUB = 4
CHUNK = 2
MESH = pl.DeviceIdType.MESH


def transport_kernel(
    groups, lines,
    ux_ref, uy_ref, iv_ref, field_hbm, wall_ref, infl_ref,
    out_hbm,
    local, halo, wall_halo, infl_halo, slots,
    load_sems, halo_recv, halo_send, mask_recv, mask_send, send_sems, recv_sems, local_sem,
):
    group_size, moments, rows, columns = field_hbm.shape
    span = 2 * rows
    block = columns // groups
    chunks = group_size // CHUNK
    me = lax.axis_index("sec")
    row = lax.axis_index("space")
    has_west = (row + lines - 1) // lines
    has_east = 1 - row // (lines - 1)
    west = (me, row - 1)
    east = (me, row + 1)
    first = pl.ds(0, SUB)
    last = pl.ds(SUB, SUB)

    loads = []
    for c in range(chunks):
        part = pl.ds(c * CHUNK, CHUNK)
        load = pltpu.make_async_copy(field_hbm.at[part], local.at[part], load_sems.at[c])
        load.start()
        loads.append(load)

    @pl.when(row == 0)
    def _():
        halo[:, :, last, :] = jnp.zeros((group_size, moments, SUB, columns), jnp.float32)
        wall_halo[last, :] = jnp.ones((SUB, columns), jnp.int32)
        infl_halo[last, :] = jnp.zeros((SUB, columns), jnp.int32)

    @pl.when(row == lines - 1)
    def _():
        halo[:, :, first, :] = jnp.zeros((group_size, moments, SUB, columns), jnp.float32)
        wall_halo[first, :] = jnp.ones((SUB, columns), jnp.int32)
        infl_halo[first, :] = jnp.zeros((SUB, columns), jnp.int32)

    barrier = pltpu.get_barrier_semaphore()
    for d in range(1, groups):
        pl.semaphore_signal(barrier, 1, device_id=(lax.rem(me + d, groups), row), device_id_type=MESH)

    @pl.when(row > 0)
    def _():
        pl.semaphore_signal(barrier, 1, device_id=west, device_id_type=MESH)

    @pl.when(row < lines - 1)
    def _():
        pl.semaphore_signal(barrier, 1, device_id=east, device_id_type=MESH)

    pl.semaphore_wait(barrier, groups - 1 + has_west + has_east)

    def halo_copy(src, dst, direction, sem_recv, sem_send):
        return pltpu.make_async_remote_copy(
            src_ref=src, dst_ref=dst, send_sem=sem_send, recv_sem=sem_recv,
            device_id=west if direction == 0 else east, device_id_type=MESH,
        )

    def field_halo(c, direction):
        part = pl.ds(c * CHUNK, CHUNK)
        if direction == 0:
            return halo_copy(field_hbm.at[part, :, first, :], halo.at[part, :, first, :], 0,
                             halo_recv.at[0, c], halo_send.at[0])
        return halo_copy(field_hbm.at[part, :, pl.ds(rows - SUB, SUB), :], halo.at[part, :, last, :], 1,
                         halo_recv.at[1, c], halo_send.at[1])

    def mask_halo(ref, store, k, direction):
        if direction == 0:
            return halo_copy(ref.at[first, :], store.at[first, :], 0, mask_recv.at[k, 0], mask_send.at[k, 0])
        return halo_copy(ref.at[pl.ds(rows - SUB, SUB), :], store.at[last, :], 1,
                         mask_recv.at[k, 1], mask_send.at[k, 1])

    @pl.when(row > 0)
    def _():
        mask_halo(wall_ref, wall_halo, 0, 0).start()
        mask_halo(infl_ref, infl_halo, 1, 0).start()
        for c in range(chunks):
            field_halo(c, 0).start()

    @pl.when(row < lines - 1)
    def _():
        mask_halo(wall_ref, wall_halo, 0, 1).start()
        mask_halo(infl_ref, infl_halo, 1, 1).start()
        for c in range(chunks):
            field_halo(c, 1).start()

    @pl.when(row < lines - 1)
    def _():
        mask_halo(wall_ref, wall_halo, 0, 0).wait_recv()
        mask_halo(infl_ref, infl_halo, 1, 0).wait_recv()

    @pl.when(row > 0)
    def _():
        mask_halo(wall_ref, wall_halo, 0, 1).wait_recv()
        mask_halo(infl_ref, infl_halo, 1, 1).wait_recv()

    def cols_of(k):
        return pl.ds(pl.multiple_of(k * block, block), block)

    for c in range(chunks):
        loads[c].wait()

        @pl.when(row < lines - 1)
        def _():
            field_halo(c, 0).wait_recv()

        @pl.when(row > 0)
        def _():
            field_halo(c, 1).wait_recv()

        def body(i, carry):
            s = c * CHUNK + i
            ux = ux_ref[s]
            uy = uy_ref[s]
            px = jnp.maximum(ux, 0.0)
            nx = jnp.minimum(ux, 0.0)
            py = jnp.maximum(uy, 0.0)
            ny = jnp.minimum(uy, 0.0)
            for m in range(moments):
                q = jnp.concatenate([local[s, m], halo[s, m]], axis=0)
                iv = iv_ref[m, s]
                for step in range(SUB):
                    col = lax.broadcasted_iota(jnp.int32, q.shape, 1)
                    western = pltpu.roll(q, 1, 0)
                    eastern = pltpu.roll(q, span - 1, 0)
                    southern = jnp.where(col == 0, 0.0, pltpu.roll(q, 1, 1))
                    northern = jnp.where(col == columns - 1, 0.0, pltpu.roll(q, columns - 1, 1))
                    t = q - px * (q - western) - nx * (eastern - q)
                    t = t - py * (q - southern) - ny * (northern - q)
                    inflow_rows = jnp.concatenate([infl_ref[...], infl_halo[...]], axis=0)
                    wall_rows = jnp.concatenate([wall_ref[...], wall_halo[...]], axis=0)
                    t = jnp.where(inflow_rows > 0, iv, t)
                    q = jnp.where(wall_rows > 0, 0.0, t)
                slots[s, m] = q[:rows]
            return carry

        lax.fori_loop(0, CHUNK, body, 0)

        part = pl.ds(c * CHUNK, CHUNK)
        for d in range(1, groups):
            k = lax.rem(me + d, groups)
            pltpu.make_async_remote_copy(
                src_ref=slots.at[part, :, :, cols_of(k)],
                dst_ref=out_hbm.at[pl.ds(me * group_size + c * CHUNK, CHUNK)],
                send_sem=send_sems.at[d - 1],
                recv_sem=recv_sems.at[d - 1],
                device_id=(k, row),
                device_id_type=MESH,
            ).start()
        pltpu.make_async_copy(
            slots.at[part, :, :, cols_of(me)],
            out_hbm.at[pl.ds(me * group_size + c * CHUNK, CHUNK)],
            local_sem,
        ).start()

    @pl.when(row > 0)
    def _():
        mask_halo(wall_ref, wall_halo, 0, 0).wait_send()
        mask_halo(infl_ref, infl_halo, 1, 0).wait_send()
        halo_copy(field_hbm.at[:, :, first, :], halo.at[:, :, first, :], 0,
                  halo_recv.at[0, 0], halo_send.at[0]).wait_send()

    @pl.when(row < lines - 1)
    def _():
        mask_halo(wall_ref, wall_halo, 0, 1).wait_send()
        mask_halo(infl_ref, infl_halo, 1, 1).wait_send()
        halo_copy(field_hbm.at[:, :, pl.ds(rows - SUB, SUB), :], halo.at[:, :, last, :], 1,
                  halo_recv.at[1, 0], halo_send.at[1]).wait_send()

    pltpu.make_async_copy(
        slots.at[:, :, :, cols_of(me)], out_hbm.at[pl.ds(me * group_size, group_size)], local_sem
    ).wait()
    for d in range(1, groups):
        k = lax.rem(me + d, groups)
        source = lax.rem(me + groups - d, groups)
        pltpu.make_async_remote_copy(
            src_ref=slots.at[:, :, :, cols_of(k)],
            dst_ref=out_hbm.at[pl.ds(me * group_size, group_size)],
            send_sem=send_sems.at[d - 1],
            recv_sem=recv_sems.at[d - 1],
            device_id=(k, row),
            device_id_type=MESH,
        ).wait_send()
        pltpu.make_async_remote_copy(
            src_ref=slots.at[:, :, :, cols_of(k)],
            dst_ref=out_hbm.at[pl.ds(source * group_size, group_size)],
            send_sem=send_sems.at[d - 1],
            recv_sem=recv_sems.at[d - 1],
            device_id=(k, row),
            device_id_type=MESH,
        ).wait_recv()


def transport_exchange(speed_x, speed_y, inflow_value, field, wall_rows, inflow_rows):
    groups = lax.axis_size("sec")
    lines = lax.axis_size("space")
    group_size, moments, rows, columns = field.shape
    block = columns // groups
    chunks = group_size // CHUNK
    smem = pl.BlockSpec(memory_space=pltpu.SMEM)
    vmem = pl.BlockSpec(memory_space=pltpu.VMEM)
    anywhere = pl.BlockSpec(memory_space=pl.ANY)
    flops = 60 * SUB * field.size
    return pl.pallas_call(
        functools.partial(transport_kernel, groups, lines),
        out_shape=jax.ShapeDtypeStruct((groups * group_size, moments, rows, block), jnp.float32),
        in_specs=[smem, smem, smem, anywhere, vmem, vmem],
        out_specs=anywhere,
        scratch_shapes=[
            pltpu.VMEM((group_size, moments, rows, columns), jnp.float32),
            pltpu.VMEM((group_size, moments, rows, columns), jnp.float32),
            pltpu.VMEM((rows, columns), jnp.int32),
            pltpu.VMEM((rows, columns), jnp.int32),
            pltpu.VMEM((group_size, moments, rows, columns), jnp.float32),
            pltpu.SemaphoreType.DMA((chunks,)),
            pltpu.SemaphoreType.DMA((2, chunks)),
            pltpu.SemaphoreType.DMA((2,)),
            pltpu.SemaphoreType.DMA((2, 2)),
            pltpu.SemaphoreType.DMA((2, 2)),
            pltpu.SemaphoreType.DMA((groups - 1,)),
            pltpu.SemaphoreType.DMA((groups - 1,)),
            pltpu.SemaphoreType.DMA(()),
        ],
        compiler_params=pltpu.CompilerParams(
            collective_id=0, has_side_effects=True, vmem_limit_bytes=60 * 1024 * 1024
        ),
        cost_estimate=pl.CostEstimate(
            flops=flops, bytes_accessed=4 * (field.size * 2), transcendentals=0
        ),
    )(speed_x, speed_y, inflow_value.T, field, wall_rows, inflow_rows)


def post_kernel(rate_ref, tf_ref, coef_ref, share_ref, x_ref, spray_ref, gas_ref):
    span, strip = gas_ref.shape
    rows = tf_ref.shape[0]
    moments = span // rows
    sections = coef_ref.shape[0]
    highest = lax.Precision.HIGH
    lane_rows = lax.broadcasted_iota(jnp.int32, (sections, strip), 0)
    rate = jnp.zeros((sections, strip), jnp.float32)
    for s in range(sections):
        rate = jnp.where(lane_rows == s, rate_ref[s], rate)
    remaining = []
    for r in range(rows):
        factor = rate * tf_ref[pl.ds(r, 1), :]
        for m in range(moments):
            x = x_ref[pl.ds(m * rows + r, sections, stride=span), :]
            evaporated = factor * x
            gas_ref[pl.ds(m * rows + r, 1), :] = jnp.sum(evaporated, axis=0, keepdims=True)
            remaining.append(x - evaporated)
    mass = jnp.concatenate([remaining[r * moments] for r in range(rows)], axis=1)
    merge_rate = jnp.dot(coef_ref[...], mass, precision=highest, preferred_element_type=jnp.float32)
    flux = jnp.concatenate(
        [
            remaining[r * moments + m] * merge_rate[:, r * strip : (r + 1) * strip]
            for r in range(rows)
            for m in range(moments)
        ],
        axis=1,
    )
    gained = jnp.dot(share_ref[...], flux, precision=highest, preferred_element_type=jnp.float32)
    for r in range(rows):
        for m in range(moments):
            at = (r * moments + m) * strip
            spray_ref[pl.ds(m * rows + r, sections, stride=span), :] = (
                remaining[r * moments + m] - flux[:, at : at + strip] + gained[:, at : at + strip]
            )


def evaporate_couple(cell_block, rates, thermal_factor, coefficient, share):
    sections, moments, rows, block = cell_block.shape
    strip = 128
    span = moments * rows
    flat = cell_block.reshape(sections * span, block)
    full = lambda shape: pl.BlockSpec(shape, lambda i: (0, 0))
    spray, gas = pl.pallas_call(
        post_kernel,
        grid=(block // strip,),
        in_specs=[
            pl.BlockSpec(memory_space=pltpu.SMEM),
            pl.BlockSpec((rows, strip), lambda i: (0, i)),
            full((sections, sections)),
            full((sections, sections)),
            pl.BlockSpec((sections * span, strip), lambda i: (0, i)),
        ],
        out_specs=[
            pl.BlockSpec((sections * span, strip), lambda i: (0, i)),
            pl.BlockSpec((span, strip), lambda i: (0, i)),
        ],
        out_shape=[
            jax.ShapeDtypeStruct((sections * span, block), jnp.float32),
            jax.ShapeDtypeStruct((span, block), jnp.float32),
        ],
        cost_estimate=pl.CostEstimate(
            flops=2 * sections * sections * flat.size // sections * (moments + 1) // moments * 6,
            bytes_accessed=8 * flat.size, transcendentals=0,
        ),
    )(rates, thermal_factor, coefficient, share, flat)
    return spray.reshape(sections, moments, rows, block), gas.reshape(moments, rows, block)


def shards(
    droplet_integrals,
    flow_number_lengthwise,
    flow_number_crosswise,
    inflow_boundary_integrals,
    boundary_wall_indicator,
    inflow_indicator,
    collision_coefficient,
    collision_target_share,
    evaporation_speed_stepwise,
    thermal_factor,
):
    cell_block = transport_exchange(
        flow_number_lengthwise, flow_number_crosswise, inflow_boundary_integrals,
        droplet_integrals, boundary_wall_indicator, inflow_indicator,
    )
    spray, gas_source = evaporate_couple(
        cell_block, evaporation_speed_stepwise, thermal_factor,
        collision_coefficient, collision_target_share,
    )
    return (spray, gas_source)


def solution(mesh):
    return jax.shard_map(
        shards,
        mesh=mesh,
        in_specs=(
            P("sec", None, "space", None),
            P("sec"),
            P("sec"),
            P("sec", None),
            P("space", None),
            P("space", None),
            P(),
            P(),
            P(),
            P("space", "sec"),
        ),
        out_specs=(P(None, None, "space", "sec"), P(None, "space", "sec")),
        check_vma=False,
    )
```

```python
import functools

import jax
import jax.numpy as jnp
from jax import lax
from jax.experimental import pallas as pl
from jax.experimental.pallas import tpu as pltpu
from jax.sharding import PartitionSpec as P

SUB = 4
CHUNK = 2
AHEAD = 2
MESH = pl.DeviceIdType.MESH


def transport_kernel(
    groups, lines,
    ux_ref, uy_ref, iv_ref, field_hbm, wall_ref, infl_ref,
    out_hbm,
    local, halo, wall_halo, infl_halo, slots,
    load_sems, halo_recv, halo_send, mask_recv, mask_send, send_sems, recv_sems, local_sem,
):
    group_size, moments, rows, columns = field_hbm.shape
    span = 2 * rows
    block = columns // groups
    chunks = group_size // CHUNK
    me = lax.axis_index("sec")
    row = lax.axis_index("space")
    has_west = (row + lines - 1) // lines
    has_east = 1 - row // (lines - 1)
    west = (me, row - 1)
    east = (me, row + 1)
    first = pl.ds(0, SUB)
    last = pl.ds(SUB, SUB)

    loads = []
    for c in range(chunks):
        part = pl.ds(c * CHUNK, CHUNK)
        load = pltpu.make_async_copy(field_hbm.at[part], local.at[part], load_sems.at[c])
        load.start()
        loads.append(load)

    @pl.when(row == 0)
    def _():
        halo[:, :, last, :] = jnp.zeros((group_size, moments, SUB, columns), jnp.float32)
        wall_halo[last, :] = jnp.ones((SUB, columns), jnp.int32)
        infl_halo[last, :] = jnp.zeros((SUB, columns), jnp.int32)

    @pl.when(row == lines - 1)
    def _():
        halo[:, :, first, :] = jnp.zeros((group_size, moments, SUB, columns), jnp.float32)
        wall_halo[first, :] = jnp.ones((SUB, columns), jnp.int32)
        infl_halo[first, :] = jnp.zeros((SUB, columns), jnp.int32)

    barrier = pltpu.get_barrier_semaphore()
    for d in range(1, groups):
        pl.semaphore_signal(barrier, 1, device_id=(lax.rem(me + d, groups), row), device_id_type=MESH)

    @pl.when(row > 0)
    def _():
        pl.semaphore_signal(barrier, 1, device_id=west, device_id_type=MESH)

    @pl.when(row < lines - 1)
    def _():
        pl.semaphore_signal(barrier, 1, device_id=east, device_id_type=MESH)

    pl.semaphore_wait(barrier, groups - 1 + has_west + has_east)

    def halo_copy(src, dst, direction, sem_recv, sem_send):
        return pltpu.make_async_remote_copy(
            src_ref=src, dst_ref=dst, send_sem=sem_send, recv_sem=sem_recv,
            device_id=west if direction == 0 else east, device_id_type=MESH,
        )

    def field_halo(c, direction):
        part = pl.ds(c * CHUNK, CHUNK)
        if direction == 0:
            return halo_copy(field_hbm.at[part, :, first, :], halo.at[part, :, first, :], 0,
                             halo_recv.at[0, c], halo_send.at[0])
        return halo_copy(field_hbm.at[part, :, pl.ds(rows - SUB, SUB), :], halo.at[part, :, last, :], 1,
                         halo_recv.at[1, c], halo_send.at[1])

    def mask_halo(ref, store, k, direction):
        if direction == 0:
            return halo_copy(ref.at[first, :], store.at[first, :], 0, mask_recv.at[k, 0], mask_send.at[k, 0])
        return halo_copy(ref.at[pl.ds(rows - SUB, SUB), :], store.at[last, :], 1,
                         mask_recv.at[k, 1], mask_send.at[k, 1])

    def send_halos(c):
        @pl.when(row > 0)
        def _():
            field_halo(c, 0).start()

        @pl.when(row < lines - 1)
        def _():
            field_halo(c, 1).start()

    @pl.when(row > 0)
    def _():
        mask_halo(wall_ref, wall_halo, 0, 0).start()
        mask_halo(infl_ref, infl_halo, 1, 0).start()

    @pl.when(row < lines - 1)
    def _():
        mask_halo(wall_ref, wall_halo, 0, 1).start()
        mask_halo(infl_ref, infl_halo, 1, 1).start()

    for c in range(min(AHEAD, chunks)):
        send_halos(c)

    @pl.when(row < lines - 1)
    def _():
        mask_halo(wall_ref, wall_halo, 0, 0).wait_recv()
        mask_halo(infl_ref, infl_halo, 1, 0).wait_recv()

    @pl.when(row > 0)
    def _():
        mask_halo(wall_ref, wall_halo, 0, 1).wait_recv()
        mask_halo(infl_ref, infl_halo, 1, 1).wait_recv()

    def cols_of(k):
        return pl.ds(pl.multiple_of(k * block, block), block)

    for c in range(chunks):
        if c + AHEAD < chunks:
            send_halos(c + AHEAD)
        loads[c].wait()

        @pl.when(row < lines - 1)
        def _():
            field_halo(c, 0).wait_recv()

        @pl.when(row > 0)
        def _():
            field_halo(c, 1).wait_recv()

        def body(i, carry):
            s = c * CHUNK + i
            ux = ux_ref[s]
            uy = uy_ref[s]
            px = jnp.maximum(ux, 0.0)
            nx = jnp.minimum(ux, 0.0)
            py = jnp.maximum(uy, 0.0)
            ny = jnp.minimum(uy, 0.0)
            for m in range(moments):
                q = jnp.concatenate([local[s, m], halo[s, m]], axis=0)
                iv = iv_ref[m, s]
                for step in range(SUB):
                    col = lax.broadcasted_iota(jnp.int32, q.shape, 1)
                    western = pltpu.roll(q, 1, 0)
                    eastern = pltpu.roll(q, span - 1, 0)
                    southern = jnp.where(col == 0, 0.0, pltpu.roll(q, 1, 1))
                    northern = jnp.where(col == columns - 1, 0.0, pltpu.roll(q, columns - 1, 1))
                    t = q - px * (q - western) - nx * (eastern - q)
                    t = t - py * (q - southern) - ny * (northern - q)
                    inflow_rows = jnp.concatenate([infl_ref[...], infl_halo[...]], axis=0)
                    wall_rows = jnp.concatenate([wall_ref[...], wall_halo[...]], axis=0)
                    t = jnp.where(inflow_rows > 0, iv, t)
                    q = jnp.where(wall_rows > 0, 0.0, t)
                slots[s, m] = q[:rows]
            return carry

        lax.fori_loop(0, CHUNK, body, 0)

        part = pl.ds(c * CHUNK, CHUNK)
        for d in range(1, groups):
            k = lax.rem(me + d, groups)
            pltpu.make_async_remote_copy(
                src_ref=slots.at[part, :, :, cols_of(k)],
                dst_ref=out_hbm.at[pl.ds(me * group_size + c * CHUNK, CHUNK)],
                send_sem=send_sems.at[d - 1],
                recv_sem=recv_sems.at[d - 1],
                device_id=(k, row),
                device_id_type=MESH,
            ).start()
        pltpu.make_async_copy(
            slots.at[part, :, :, cols_of(me)],
            out_hbm.at[pl.ds(me * group_size + c * CHUNK, CHUNK)],
            local_sem,
        ).start()

    @pl.when(row > 0)
    def _():
        mask_halo(wall_ref, wall_halo, 0, 0).wait_send()
        mask_halo(infl_ref, infl_halo, 1, 0).wait_send()
        halo_copy(field_hbm.at[:, :, first, :], halo.at[:, :, first, :], 0,
                  halo_recv.at[0, 0], halo_send.at[0]).wait_send()

    @pl.when(row < lines - 1)
    def _():
        mask_halo(wall_ref, wall_halo, 0, 1).wait_send()
        mask_halo(infl_ref, infl_halo, 1, 1).wait_send()
        halo_copy(field_hbm.at[:, :, pl.ds(rows - SUB, SUB), :], halo.at[:, :, last, :], 1,
                  halo_recv.at[1, 0], halo_send.at[1]).wait_send()

    pltpu.make_async_copy(
        slots.at[:, :, :, cols_of(me)], out_hbm.at[pl.ds(me * group_size, group_size)], local_sem
    ).wait()
    for d in range(1, groups):
        k = lax.rem(me + d, groups)
        source = lax.rem(me + groups - d, groups)
        pltpu.make_async_remote_copy(
            src_ref=slots.at[:, :, :, cols_of(k)],
            dst_ref=out_hbm.at[pl.ds(me * group_size, group_size)],
            send_sem=send_sems.at[d - 1],
            recv_sem=recv_sems.at[d - 1],
            device_id=(k, row),
            device_id_type=MESH,
        ).wait_send()
        pltpu.make_async_remote_copy(
            src_ref=slots.at[:, :, :, cols_of(k)],
            dst_ref=out_hbm.at[pl.ds(source * group_size, group_size)],
            send_sem=send_sems.at[d - 1],
            recv_sem=recv_sems.at[d - 1],
            device_id=(k, row),
            device_id_type=MESH,
        ).wait_recv()


def transport_exchange(speed_x, speed_y, inflow_value, field, wall_rows, inflow_rows):
    groups = lax.axis_size("sec")
    lines = lax.axis_size("space")
    group_size, moments, rows, columns = field.shape
    block = columns // groups
    chunks = group_size // CHUNK
    smem = pl.BlockSpec(memory_space=pltpu.SMEM)
    vmem = pl.BlockSpec(memory_space=pltpu.VMEM)
    anywhere = pl.BlockSpec(memory_space=pl.ANY)
    flops = 60 * SUB * field.size
    return pl.pallas_call(
        functools.partial(transport_kernel, groups, lines),
        out_shape=jax.ShapeDtypeStruct((groups * group_size, moments, rows, block), jnp.float32),
        in_specs=[smem, smem, smem, anywhere, vmem, vmem],
        out_specs=anywhere,
        scratch_shapes=[
            pltpu.VMEM((group_size, moments, rows, columns), jnp.float32),
            pltpu.VMEM((group_size, moments, rows, columns), jnp.float32),
            pltpu.VMEM((rows, columns), jnp.int32),
            pltpu.VMEM((rows, columns), jnp.int32),
            pltpu.VMEM((group_size, moments, rows, columns), jnp.float32),
            pltpu.SemaphoreType.DMA((chunks,)),
            pltpu.SemaphoreType.DMA((2, chunks)),
            pltpu.SemaphoreType.DMA((2,)),
            pltpu.SemaphoreType.DMA((2, 2)),
            pltpu.SemaphoreType.DMA((2, 2)),
            pltpu.SemaphoreType.DMA((groups - 1,)),
            pltpu.SemaphoreType.DMA((groups - 1,)),
            pltpu.SemaphoreType.DMA(()),
        ],
        compiler_params=pltpu.CompilerParams(
            collective_id=0, has_side_effects=True, vmem_limit_bytes=60 * 1024 * 1024
        ),
        cost_estimate=pl.CostEstimate(
            flops=flops, bytes_accessed=4 * (field.size * 2), transcendentals=0
        ),
    )(speed_x, speed_y, inflow_value.T, field, wall_rows, inflow_rows)


def post_kernel(rate_ref, tf_ref, coef_ref, share_ref, x_ref, spray_ref, gas_ref):
    span, strip = gas_ref.shape
    rows = tf_ref.shape[0]
    moments = span // rows
    sections = coef_ref.shape[0]
    highest = lax.Precision.HIGH
    lane_rows = lax.broadcasted_iota(jnp.int32, (sections, strip), 0)
    rate = jnp.zeros((sections, strip), jnp.float32)
    for s in range(sections):
        rate = jnp.where(lane_rows == s, rate_ref[s], rate)
    remaining = []
    for r in range(rows):
        factor = rate * tf_ref[pl.ds(r, 1), :]
        for m in range(moments):
            x = x_ref[pl.ds(m * rows + r, sections, stride=span), :]
            evaporated = factor * x
            gas_ref[pl.ds(m * rows + r, 1), :] = jnp.sum(evaporated, axis=0, keepdims=True)
            remaining.append(x - evaporated)
    mass = jnp.concatenate([remaining[r * moments] for r in range(rows)], axis=1)
    merge_rate = jnp.dot(coef_ref[...], mass, precision=highest, preferred_element_type=jnp.float32)
    flux = jnp.concatenate(
        [
            remaining[r * moments + m] * merge_rate[:, r * strip : (r + 1) * strip]
            for r in range(rows)
            for m in range(moments)
        ],
        axis=1,
    )
    gained = jnp.dot(share_ref[...], flux, precision=highest, preferred_element_type=jnp.float32)
    for r in range(rows):
        for m in range(moments):
            at = (r * moments + m) * strip
            spray_ref[pl.ds(m * rows + r, sections, stride=span), :] = (
                remaining[r * moments + m] - flux[:, at : at + strip] + gained[:, at : at + strip]
            )


def evaporate_couple(cell_block, rates, thermal_factor, coefficient, share):
    sections, moments, rows, block = cell_block.shape
    strip = 128
    span = moments * rows
    flat = cell_block.reshape(sections * span, block)
    full = lambda shape: pl.BlockSpec(shape, lambda i: (0, 0))
    spray, gas = pl.pallas_call(
        post_kernel,
        grid=(block // strip,),
        in_specs=[
            pl.BlockSpec(memory_space=pltpu.SMEM),
            pl.BlockSpec((rows, strip), lambda i: (0, i)),
            full((sections, sections)),
            full((sections, sections)),
            pl.BlockSpec((sections * span, strip), lambda i: (0, i)),
        ],
        out_specs=[
            pl.BlockSpec((sections * span, strip), lambda i: (0, i)),
            pl.BlockSpec((span, strip), lambda i: (0, i)),
        ],
        out_shape=[
            jax.ShapeDtypeStruct((sections * span, block), jnp.float32),
            jax.ShapeDtypeStruct((span, block), jnp.float32),
        ],
        cost_estimate=pl.CostEstimate(
            flops=2 * sections * sections * flat.size // sections * (moments + 1) // moments * 6,
            bytes_accessed=8 * flat.size, transcendentals=0,
        ),
    )(rates, thermal_factor, coefficient, share, flat)
    return spray.reshape(sections, moments, rows, block), gas.reshape(moments, rows, block)


def shards(
    droplet_integrals,
    flow_number_lengthwise,
    flow_number_crosswise,
    inflow_boundary_integrals,
    boundary_wall_indicator,
    inflow_indicator,
    collision_coefficient,
    collision_target_share,
    evaporation_speed_stepwise,
    thermal_factor,
):
    cell_block = transport_exchange(
        flow_number_lengthwise, flow_number_crosswise, inflow_boundary_integrals,
        droplet_integrals, boundary_wall_indicator, inflow_indicator,
    )
    spray, gas_source = evaporate_couple(
        cell_block, evaporation_speed_stepwise, thermal_factor,
        collision_coefficient, collision_target_share,
    )
    return (spray, gas_source)


def solution(mesh):
    return jax.shard_map(
        shards,
        mesh=mesh,
        in_specs=(
            P("sec", None, "space", None),
            P("sec"),
            P("sec"),
            P("sec", None),
            P("space", None),
            P("space", None),
            P(),
            P(),
            P(),
            P("space", "sec"),
        ),
        out_specs=(P(None, None, "space", "sec"), P(None, "space", "sec")),
        check_vma=False,
    )
```

```python
import functools

import jax
import jax.numpy as jnp
from jax import lax
from jax.experimental import pallas as pl
from jax.experimental.pallas import tpu as pltpu
from jax.sharding import PartitionSpec as P

SUB = 4
CHUNK = 4
RELAYED = (2, 3)
PLANE = 4
MESH = pl.DeviceIdType.MESH


def transport_kernel(
    groups, lines,
    ux_ref, uy_ref, iv_ref, field_hbm, wall_ref, infl_ref,
    out_hbm,
    local, halo, wall_halo, infl_halo, slots, relay,
    load_sems, halo_recv, halo_send, mask_recv, mask_send, send_sems, recv_sems, local_sem,
    relay_recv, relay_send,
):
    group_size, moments, rows, columns = field_hbm.shape
    span = 2 * rows
    block = columns // groups
    chunks = group_size // CHUNK
    me = lax.axis_index("sec")
    row = lax.axis_index("space")
    has_west = (row + lines - 1) // lines
    has_east = 1 - row // (lines - 1)
    west = (me, row - 1)
    east = (me, row + 1)
    first = pl.ds(0, SUB)
    last = pl.ds(SUB, SUB)
    res = row % PLANE
    edge_low = (res == PLANE - 1) & (row < lines - 1)
    edge_high = (res == 0) & (row > 0)
    relay_low = (res == PLANE - 2) & (row + 2 < lines)
    relay_high = (res == 1) & (row >= PLANE + 1)

    loads = []
    for c in range(chunks):
        part = pl.ds(c * CHUNK, CHUNK)
        load = pltpu.make_async_copy(field_hbm.at[part], local.at[part], load_sems.at[c])
        load.start()
        loads.append(load)

    @pl.when(row == 0)
    def _():
        halo[:, :, last, :] = jnp.zeros((group_size, moments, SUB, columns), jnp.float32)
        wall_halo[last, :] = jnp.ones((SUB, columns), jnp.int32)
        infl_halo[last, :] = jnp.zeros((SUB, columns), jnp.int32)

    @pl.when(row == lines - 1)
    def _():
        halo[:, :, first, :] = jnp.zeros((group_size, moments, SUB, columns), jnp.float32)
        wall_halo[first, :] = jnp.ones((SUB, columns), jnp.int32)
        infl_halo[first, :] = jnp.zeros((SUB, columns), jnp.int32)

    barrier = pltpu.get_barrier_semaphore()
    for d in range(1, groups):
        pl.semaphore_signal(barrier, 1, device_id=(lax.rem(me + d, groups), row), device_id_type=MESH)

    @pl.when(row > 0)
    def _():
        pl.semaphore_signal(barrier, 1, device_id=west, device_id_type=MESH)

    @pl.when(row < lines - 1)
    def _():
        pl.semaphore_signal(barrier, 1, device_id=east, device_id_type=MESH)

    for d in range(1, groups):
        partner = lax.rem(me + d, groups)
        for cond, offset in ((relay_low, 1), (relay_high, -1), (edge_low, -1), (edge_high, 1)):
            @pl.when(cond)
            def _():
                pl.semaphore_signal(barrier, 1, device_id=(partner, row + offset), device_id_type=MESH)
    same = lambda v: 1 - ((res - v + PLANE) % PLANE + PLANE - 1) // PLANE
    past = lambda a: (row - a + lines) // lines
    crossing = (
        same(PLANE - 1) * has_east + same(0) * has_west
        + same(PLANE - 2) * (1 - past(lines - 2)) + same(1) * past(PLANE + 1)
    )
    pl.semaphore_wait(barrier, groups - 1 + has_west + has_east + (groups - 1) * crossing)

    def halo_copy(src, dst, direction, sem_recv, sem_send):
        return pltpu.make_async_remote_copy(
            src_ref=src, dst_ref=dst, send_sem=sem_send, recv_sem=sem_recv,
            device_id=west if direction == 0 else east, device_id_type=MESH,
        )

    def field_halo(c, direction):
        part = pl.ds(c * CHUNK, CHUNK)
        if direction == 0:
            return halo_copy(field_hbm.at[part, :, first, :], halo.at[part, :, first, :], 0,
                             halo_recv.at[0, c], halo_send.at[0])
        return halo_copy(field_hbm.at[part, :, pl.ds(rows - SUB, SUB), :], halo.at[part, :, last, :], 1,
                         halo_recv.at[1, c], halo_send.at[1])

    def mask_halo(ref, store, k, direction):
        if direction == 0:
            return halo_copy(ref.at[first, :], store.at[first, :], 0, mask_recv.at[k, 0], mask_send.at[k, 0])
        return halo_copy(ref.at[pl.ds(rows - SUB, SUB), :], store.at[last, :], 1,
                         mask_recv.at[k, 1], mask_send.at[k, 1])

    @pl.when(row > 0)
    def _():
        mask_halo(wall_ref, wall_halo, 0, 0).start()
        mask_halo(infl_ref, infl_halo, 1, 0).start()
        for c in range(chunks):
            field_halo(c, 0).start()

    @pl.when(row < lines - 1)
    def _():
        mask_halo(wall_ref, wall_halo, 0, 1).start()
        mask_halo(infl_ref, infl_halo, 1, 1).start()
        for c in range(chunks):
            field_halo(c, 1).start()

    @pl.when(row < lines - 1)
    def _():
        mask_halo(wall_ref, wall_halo, 0, 0).wait_recv()
        mask_halo(infl_ref, infl_halo, 1, 0).wait_recv()

    @pl.when(row > 0)
    def _():
        mask_halo(wall_ref, wall_halo, 0, 1).wait_recv()
        mask_halo(infl_ref, infl_halo, 1, 1).wait_recv()

    def cols_of(k):
        return pl.ds(pl.multiple_of(k * block, block), block)

    def forward(offset, j):
        c = RELAYED[j]
        for d in range(1, groups):
            pltpu.make_async_remote_copy(
                src_ref=slots.at[pl.ds(0, CHUNK), :, :, cols_of(me)],
                dst_ref=relay.at[0, j, d - 1],
                send_sem=relay_send.at[0],
                recv_sem=relay_recv.at[0, j, d - 1],
                device_id=(me, row + offset),
                device_id_type=MESH,
            ).wait_recv()
            pltpu.make_async_remote_copy(
                src_ref=relay.at[0, j, d - 1],
                dst_ref=out_hbm.at[pl.ds(me * group_size + c * CHUNK, CHUNK)],
                send_sem=relay_send.at[0],
                recv_sem=recv_sems.at[d - 1],
                device_id=(lax.rem(me + d, groups), row + offset),
                device_id_type=MESH,
            ).start()


    for c in range(chunks):
        if c == chunks - 1:
            for j in range(len(RELAYED) - 1):
                pl.when(relay_low)(functools.partial(forward, 1, j))
                pl.when(relay_high)(functools.partial(forward, -1, j))
        loads[c].wait()

        @pl.when(row < lines - 1)
        def _():
            field_halo(c, 0).wait_recv()

        @pl.when(row > 0)
        def _():
            field_halo(c, 1).wait_recv()

        def body(i, carry):
            s = c * CHUNK + i
            ux = ux_ref[s]
            uy = uy_ref[s]
            px = jnp.maximum(ux, 0.0)
            nx = jnp.minimum(ux, 0.0)
            py = jnp.maximum(uy, 0.0)
            ny = jnp.minimum(uy, 0.0)
            for m in range(moments):
                q = jnp.concatenate([local[s, m], halo[s, m]], axis=0)
                iv = iv_ref[m, s]
                for step in range(SUB):
                    col = lax.broadcasted_iota(jnp.int32, q.shape, 1)
                    western = pltpu.roll(q, 1, 0)
                    eastern = pltpu.roll(q, span - 1, 0)
                    southern = jnp.where(col == 0, 0.0, pltpu.roll(q, 1, 1))
                    northern = jnp.where(col == columns - 1, 0.0, pltpu.roll(q, columns - 1, 1))
                    t = q - px * (q - western) - nx * (eastern - q)
                    t = t - py * (q - southern) - ny * (northern - q)
                    inflow_rows = jnp.concatenate([infl_ref[...], infl_halo[...]], axis=0)
                    wall_rows = jnp.concatenate([wall_ref[...], wall_halo[...]], axis=0)
                    t = jnp.where(inflow_rows > 0, iv, t)
                    q = jnp.where(wall_rows > 0, 0.0, t)
                slots[s, m] = q[:rows]
            return carry

        lax.fori_loop(0, CHUNK, body, 0)

        part = pl.ds(c * CHUNK, CHUNK)

        def direct():
            for d in range(1, groups):
                k = lax.rem(me + d, groups)
                pltpu.make_async_remote_copy(
                    src_ref=slots.at[part, :, :, cols_of(k)],
                    dst_ref=out_hbm.at[pl.ds(me * group_size + c * CHUNK, CHUNK)],
                    send_sem=send_sems.at[d - 1],
                    recv_sem=recv_sems.at[d - 1],
                    device_id=(k, row),
                    device_id_type=MESH,
                ).start()

        if c in RELAYED:
            j = RELAYED.index(c)

            def via(offset):
                for d in range(1, groups):
                    k = lax.rem(me + d, groups)
                    pltpu.make_async_remote_copy(
                        src_ref=slots.at[part, :, :, cols_of(k)],
                        dst_ref=relay.at[0, j, d - 1],
                        send_sem=send_sems.at[d - 1],
                        recv_sem=relay_recv.at[0, j, d - 1],
                        device_id=(me, row + offset),
                        device_id_type=MESH,
                    ).start()

            pl.when(edge_low)(lambda: via(-1))
            pl.when(edge_high)(lambda: via(1))
            pl.when(jnp.logical_not(edge_low | edge_high))(direct)
        else:
            direct()
        pltpu.make_async_copy(
            slots.at[part, :, :, cols_of(me)],
            out_hbm.at[pl.ds(me * group_size + c * CHUNK, CHUNK)],
            local_sem,
        ).start()

    pl.when(relay_low)(lambda: forward(1, len(RELAYED) - 1))
    pl.when(relay_high)(lambda: forward(-1, len(RELAYED) - 1))

    def settle(offset):
        pltpu.make_async_remote_copy(
            src_ref=relay.at[0], dst_ref=relay.at[0],
            send_sem=relay_send.at[0], recv_sem=relay_recv.at[0, 0, 0],
            device_id=(me, row + offset), device_id_type=MESH,
        ).wait_send()

    pl.when(relay_low)(lambda: settle(1))
    pl.when(relay_high)(lambda: settle(-1))


    @pl.when(row > 0)
    def _():
        mask_halo(wall_ref, wall_halo, 0, 0).wait_send()
        mask_halo(infl_ref, infl_halo, 1, 0).wait_send()
        halo_copy(field_hbm.at[:, :, first, :], halo.at[:, :, first, :], 0,
                  halo_recv.at[0, 0], halo_send.at[0]).wait_send()

    @pl.when(row < lines - 1)
    def _():
        mask_halo(wall_ref, wall_halo, 0, 1).wait_send()
        mask_halo(infl_ref, infl_halo, 1, 1).wait_send()
        halo_copy(field_hbm.at[:, :, pl.ds(rows - SUB, SUB), :], halo.at[:, :, last, :], 1,
                  halo_recv.at[1, 0], halo_send.at[1]).wait_send()

    pltpu.make_async_copy(
        slots.at[:, :, :, cols_of(me)], out_hbm.at[pl.ds(me * group_size, group_size)], local_sem
    ).wait()
    for d in range(1, groups):
        k = lax.rem(me + d, groups)
        source = lax.rem(me + groups - d, groups)
        pltpu.make_async_remote_copy(
            src_ref=slots.at[:, :, :, cols_of(k)],
            dst_ref=out_hbm.at[pl.ds(me * group_size, group_size)],
            send_sem=send_sems.at[d - 1],
            recv_sem=recv_sems.at[d - 1],
            device_id=(k, row),
            device_id_type=MESH,
        ).wait_send()
        pltpu.make_async_remote_copy(
            src_ref=slots.at[:, :, :, cols_of(k)],
            dst_ref=out_hbm.at[pl.ds(source * group_size, group_size)],
            send_sem=send_sems.at[d - 1],
            recv_sem=recv_sems.at[d - 1],
            device_id=(k, row),
            device_id_type=MESH,
        ).wait_recv()


def transport_exchange(speed_x, speed_y, inflow_value, field, wall_rows, inflow_rows):
    groups = lax.axis_size("sec")
    lines = lax.axis_size("space")
    group_size, moments, rows, columns = field.shape
    block = columns // groups
    chunks = group_size // CHUNK
    smem = pl.BlockSpec(memory_space=pltpu.SMEM)
    vmem = pl.BlockSpec(memory_space=pltpu.VMEM)
    anywhere = pl.BlockSpec(memory_space=pl.ANY)
    flops = 60 * SUB * field.size
    return pl.pallas_call(
        functools.partial(transport_kernel, groups, lines),
        out_shape=jax.ShapeDtypeStruct((groups * group_size, moments, rows, block), jnp.float32),
        in_specs=[smem, smem, smem, anywhere, vmem, vmem],
        out_specs=anywhere,
        scratch_shapes=[
            pltpu.VMEM((group_size, moments, rows, columns), jnp.float32),
            pltpu.VMEM((group_size, moments, rows, columns), jnp.float32),
            pltpu.VMEM((rows, columns), jnp.int32),
            pltpu.VMEM((rows, columns), jnp.int32),
            pltpu.VMEM((group_size, moments, rows, columns), jnp.float32),
            pltpu.VMEM((1, len(RELAYED), groups - 1, CHUNK, moments, rows, block), jnp.float32),
            pltpu.SemaphoreType.DMA((chunks,)),
            pltpu.SemaphoreType.DMA((2, chunks)),
            pltpu.SemaphoreType.DMA((2,)),
            pltpu.SemaphoreType.DMA((2, 2)),
            pltpu.SemaphoreType.DMA((2, 2)),
            pltpu.SemaphoreType.DMA((groups - 1,)),
            pltpu.SemaphoreType.DMA((groups - 1,)),
            pltpu.SemaphoreType.DMA(()),
            pltpu.SemaphoreType.DMA((1, len(RELAYED), groups - 1)),
            pltpu.SemaphoreType.DMA((1,)),
        ],
        compiler_params=pltpu.CompilerParams(
            collective_id=0, has_side_effects=True, vmem_limit_bytes=60 * 1024 * 1024
        ),
        cost_estimate=pl.CostEstimate(
            flops=flops, bytes_accessed=4 * (field.size * 2), transcendentals=0
        ),
    )(speed_x, speed_y, inflow_value.T, field, wall_rows, inflow_rows)


def post_kernel(rate_ref, tf_ref, coef_ref, share_ref, x_ref, spray_ref, gas_ref):
    span, strip = gas_ref.shape
    rows = tf_ref.shape[0]
    moments = span // rows
    sections = coef_ref.shape[0]
    highest = lax.Precision.HIGH
    lane_rows = lax.broadcasted_iota(jnp.int32, (sections, strip), 0)
    rate = jnp.zeros((sections, strip), jnp.float32)
    for s in range(sections):
        rate = jnp.where(lane_rows == s, rate_ref[s], rate)
    remaining = []
    for r in range(rows):
        factor = rate * tf_ref[pl.ds(r, 1), :]
        for m in range(moments):
            x = x_ref[pl.ds(m * rows + r, sections, stride=span), :]
            evaporated = factor * x
            gas_ref[pl.ds(m * rows + r, 1), :] = jnp.sum(evaporated, axis=0, keepdims=True)
            remaining.append(x - evaporated)
    mass = jnp.concatenate([remaining[r * moments] for r in range(rows)], axis=1)
    merge_rate = jnp.dot(coef_ref[...], mass, precision=highest, preferred_element_type=jnp.float32)
    flux = jnp.concatenate(
        [
            remaining[r * moments + m] * merge_rate[:, r * strip : (r + 1) * strip]
            for r in range(rows)
            for m in range(moments)
        ],
        axis=1,
    )
    gained = jnp.dot(share_ref[...], flux, precision=highest, preferred_element_type=jnp.float32)
    for r in range(rows):
        for m in range(moments):
            at = (r * moments + m) * strip
            spray_ref[pl.ds(m * rows + r, sections, stride=span), :] = (
                remaining[r * moments + m] - flux[:, at : at + strip] + gained[:, at : at + strip]
            )


def evaporate_couple(cell_block, rates, thermal_factor, coefficient, share):
    sections, moments, rows, block = cell_block.shape
    strip = 128
    span = moments * rows
    flat = cell_block.reshape(sections * span, block)
    full = lambda shape: pl.BlockSpec(shape, lambda i: (0, 0))
    spray, gas = pl.pallas_call(
        post_kernel,
        grid=(block // strip,),
        in_specs=[
            pl.BlockSpec(memory_space=pltpu.SMEM),
            pl.BlockSpec((rows, strip), lambda i: (0, i)),
            full((sections, sections)),
            full((sections, sections)),
            pl.BlockSpec((sections * span, strip), lambda i: (0, i)),
        ],
        out_specs=[
            pl.BlockSpec((sections * span, strip), lambda i: (0, i)),
            pl.BlockSpec((span, strip), lambda i: (0, i)),
        ],
        out_shape=[
            jax.ShapeDtypeStruct((sections * span, block), jnp.float32),
            jax.ShapeDtypeStruct((span, block), jnp.float32),
        ],
        cost_estimate=pl.CostEstimate(
            flops=2 * sections * sections * flat.size // sections * (moments + 1) // moments * 6,
            bytes_accessed=8 * flat.size, transcendentals=0,
        ),
    )(rates, thermal_factor, coefficient, share, flat)
    return spray.reshape(sections, moments, rows, block), gas.reshape(moments, rows, block)


def shards(
    droplet_integrals,
    flow_number_lengthwise,
    flow_number_crosswise,
    inflow_boundary_integrals,
    boundary_wall_indicator,
    inflow_indicator,
    collision_coefficient,
    collision_target_share,
    evaporation_speed_stepwise,
    thermal_factor,
):
    cell_block = transport_exchange(
        flow_number_lengthwise, flow_number_crosswise, inflow_boundary_integrals,
        droplet_integrals, boundary_wall_indicator, inflow_indicator,
    )
    spray, gas_source = evaporate_couple(
        cell_block, evaporation_speed_stepwise, thermal_factor,
        collision_coefficient, collision_target_share,
    )
    return (spray, gas_source)


def solution(mesh):
    return jax.shard_map(
        shards,
        mesh=mesh,
        in_specs=(
            P("sec", None, "space", None),
            P("sec"),
            P("sec"),
            P("sec", None),
            P("space", None),
            P("space", None),
            P(),
            P(),
            P(),
            P("space", "sec"),
        ),
        out_specs=(P(None, None, "space", "sec"), P(None, "space", "sec")),
        check_vma=False,
    )
```
